32 devices in a mesh: rows: 8 (over z, x), cols: 4 (over y, core).
Axes of the slice: x: 2, y: 2, z: 4, core: 2. Of those that a mesh axis runs over, the one named last changes fastest.
Arguments:
- row_features: float32 [4096, 64], P('rows'), may hold values from -6 to 6, as said below
- col_features: float32 [16384, 64], P('cols'), may hold values from -6 to 6, as said below
- test_block: bfloat16 [16384, 256], P('cols'), may hold values from -0.046875 to 0.046875, as said below
Outputs:
- basis: float32 [4096, 256], P('rows', 'cols')
- projected: float32 [256, 16384], P('rows', 'cols')
The draws below stay inside these ranges and needn't reach their ends.
Inputs may be any that keep to these rules, and one draw needn't show every extreme that they name: `row_features`: independent entries of mean zero and unit variance. `col_features`: independent entries of mean zero and unit variance. `test_block`: independent entries of mean zero and variance 1 / 16384.
All inputs are finite; a program needn't handle non-finite values.
Results may differ from the reference program's by a relative error of at most 0.0095.
Values may be sent and summed in bfloat16 or wider, within the bound.
No kernel may reach another device: no remote copies, remote signals or barrier semaphores. Data moves between devices by JAX's collectives and lax.ppermute only.
A program may use at most 64 MiB of HBM per device.

```python
import math
import jax
import jax.numpy as jnp
from jax import lax

F = 64
S = 256
R_DEV = 512
NR = 4096
NC = 16384


def centered(key, shape, spread):
    return spread * jax.random.truncated_normal(key, -6.0, 6.0, shape, jnp.float32)


def draw_row_features(key, part):
    return centered(jax.random.fold_in(key, 11), (NR, F), 1.0)


def draw_col_features(key, part):
    return centered(jax.random.fold_in(key, 23), (NC, F), 1.0)


def draw_test_block(key, part):
    return centered(jax.random.fold_in(key, 37), (NC, S), 1.0 / NC ** 0.5).astype(jnp.bfloat16)


def setup_inputs(seed: int = 0) -> dict:
    splits = jax.random.split(jax.random.key(seed), 4)
    return {
        "row_features": draw_row_features(jax.random.fold_in(splits[3], 71), 0),
        "col_features": draw_col_features(jax.random.fold_in(splits[3], 71), 0),
        "test_block": draw_test_block(jax.random.fold_in(splits[3], 71), 0),
    }


def kernel_tile(rows, cols):
    inner = lax.dot_general(rows.astype(jnp.float32), cols.astype(jnp.float32), (((1,), (1,)), ((), ())), precision=lax.Precision.HIGHEST, preferred_element_type=jnp.float32) * (1.0 / math.sqrt(F))
    shifted = inner + 1.0
    return (shifted * shifted * shifted).astype(jnp.bfloat16)

def reference(row_features, col_features, test_block):
    blocks = row_features.reshape(NR // R_DEV, R_DEV, F)

    def sketch_block(block):
        return jnp.dot(kernel_tile(block, col_features).astype(jnp.float32), test_block.astype(jnp.float32), preferred_element_type=jnp.float32)
    sketch = lax.map(sketch_block, blocks).reshape(NR, S)
    gram = lax.dot_general(sketch.astype(jnp.float32), sketch.astype(jnp.float32), (((0,), (0,)), ((), ())), precision=lax.Precision.HIGHEST, preferred_element_type=jnp.float32)
    lower = jnp.linalg.cholesky(gram)
    basis = jax.scipy.linalg.solve_triangular(lower, sketch.T, lower=True).T
    basis_b = basis.astype(jnp.bfloat16).reshape(NR // R_DEV, R_DEV, S)

    def accumulate(total, pair):
        block, qblock = pair
        tile = kernel_tile(block, col_features)
        part = lax.dot_general(qblock.astype(jnp.float32), tile.astype(jnp.float32), (((0,), (0,)), ((), ())), preferred_element_type=jnp.float32)
        part = lax.optimization_barrier(part.astype(jnp.bfloat16))
        return (total + part.astype(jnp.float32), None)
    projected, _ = lax.scan(accumulate, jnp.zeros((S, NC), jnp.float32), (blocks, basis_b))
    return (basis, projected)
```

```python
import math

import jax
import jax.numpy as jnp
from jax import lax
from jax.experimental import pallas as pl
from jax.experimental.pallas import tpu as pltpu
from jax.sharding import PartitionSpec as P

F32 = jnp.float32
BF16 = jnp.bfloat16
NN = ((1,), (0,))
NT = ((1,), (1,))
TN = ((0,), (0,))


def mm(a, b, dims, precision=None):
    return lax.dot_general(
        a, b, (dims, ((), ())), precision=precision, preferred_element_type=F32
    )


def split(a):
    high = a.astype(BF16)
    return high, (a - high.astype(F32)).astype(BF16)


def cube(inner):
    shifted = inner + 1.0
    return (shifted * shifted * shifted).astype(BF16)


def factor_inverse(rows, n):
    blocks = n // 8
    lane = lax.broadcasted_iota(jnp.int32, (8, n), 1)
    sub = lax.broadcasted_iota(jnp.int32, (8, n), 0)
    rows = list(rows)
    done = []

    def row_of(a, t):
        return jnp.broadcast_to(a[t : t + 1, :], (8, n))

    for g in range(blocks):
        first = 8 * g
        inside = (lane >= first) & (lane < first + 8)
        pivot = jnp.where(inside, jnp.where(lane == sub + first, 1.0, 0.0), rows[g])
        column = [
            [jnp.broadcast_to(rows[v][:, first + k : first + k + 1], (8, n)) for k in range(8)]
            for v in range(g, blocks)
        ]
        factor = [[None] * 8 for _ in range(g, blocks)]
        diagonal = jnp.zeros((8, n), F32)
        for t in range(8):
            d = row_of(column[0][t], t)
            diagonal = jnp.where(sub == t, d, diagonal)
            r = 1.0 / d
            own = jnp.where(sub > t, column[0][t] * r, 0.0)
            for v in range(1, blocks - g):
                factor[v][t] = column[v][t] * r
            for k in range(t + 1, 8):
                e = row_of(column[0][k], t)
                column[0][k] = column[0][k] - own * e
                for v in range(1, blocks - g):
                    column[v][k] = column[v][k] - factor[v][t] * e
            pivot = pivot - own * row_of(pivot, t)
        pivots = [row_of(pivot, t) for t in range(8)]
        for v in range(1, blocks - g):
            m = jnp.where(inside, 0.0, rows[g + v])
            for t in range(8):
                m = m - factor[v][t] * pivots[t]
            rows[g + v] = m
        done.append(jnp.where(lane <= sub + first, pivot, 0.0) * lax.rsqrt(diagonal))
    return jnp.concatenate(done, axis=0)


def inverse_factor(gram, base=128):
    n = gram.shape[0]
    if n <= base:
        return factor_inverse([gram[8 * i : 8 * i + 8, :] for i in range(n // 8)], n)
    k = n // 2
    high = lax.Precision.HIGHEST
    w11 = inverse_factor(gram[:k, :k], base)
    l21 = mm(gram[k:, :k], w11, NT, high)
    w22 = inverse_factor(gram[k:, k:] - mm(l21, l21, NT, high), base)
    w21 = -mm(w22, mm(l21, w11, NN, high), NN, high)
    top = jnp.concatenate([w11, jnp.zeros((k, n - k), F32)], axis=1)
    return jnp.concatenate([top, jnp.concatenate([w21, w22], axis=1)], axis=0)


def sketch_kernel(scale, x_ref, y_ref, t_ref, s_ref, y4_ref, x4):
    @pl.when(pl.program_id(0) == 0)
    def _():
        high, low = split(x_ref[...] * scale)
        x4[...] = jnp.concatenate([high, low, high, low], axis=0).T
        s_ref[...] = jnp.zeros_like(s_ref)

    high, low = split(y_ref[...])
    y4 = jnp.concatenate([high, high, low, low], axis=0)
    y4_ref[...] = y4.T
    s_ref[...] += mm(cube(mm(x4[...], y4, NN)), t_ref[...], NN)


def sketch_call(x_t, y_t, test, scale):
    width, rows = x_t.shape
    cols, columns = test.shape
    tile = 512
    return pl.pallas_call(
        lambda *refs: sketch_kernel(scale, *refs),
        grid=(cols // tile,),
        in_specs=[
            pl.BlockSpec((width, rows), lambda j: (0, 0)),
            pl.BlockSpec((width, tile), lambda j: (0, j)),
            pl.BlockSpec((tile, columns), lambda j: (j, 0)),
        ],
        out_specs=[
            pl.BlockSpec((rows, columns), lambda j: (0, 0)),
            pl.BlockSpec((tile, 4 * width), lambda j: (j, 0)),
        ],
        out_shape=[
            jax.ShapeDtypeStruct((rows, columns), F32),
            jax.ShapeDtypeStruct((cols, 4 * width), BF16),
        ],
        scratch_shapes=[pltpu.VMEM((rows, 4 * width), BF16)],
        name="sketch_tile",
    )(x_t, y_t, test)


def product_kernel(scale, first, *refs):
    if first:
        x_ref, s_ref, y4_ref, z_ref, g_ref = refs
    else:
        x_ref, s_ref, y4_ref, z_in, g_in, z_ref, g_ref = refs
    m, n = pl.program_id(0), pl.program_id(1)
    s = s_ref[...]
    high, low = split(x_ref[...] * scale)
    x4 = jnp.concatenate([high, low, high, low], axis=0)
    part = mm(cube(mm(y4_ref[...], x4, NN)), s, NN)

    @pl.when(n == 0)
    def _():
        z_ref[...] = part if first else z_in[...] + part

    @pl.when(n > 0)
    def _():
        z_ref[...] += part

    @pl.when((m == 0) & (n == 0))
    def _():
        g_ref[...] = jnp.zeros_like(g_ref) if first else g_in[...]

    @pl.when(m == 0)
    def _():
        g_ref[...] += mm(s, s, TN)


def product_call(x_t, s, y4, scale, carry=None):
    width, rows = x_t.shape
    columns = s.shape[1]
    cols = y4.shape[0]
    tile_m, tile_n = 512, min(1024, rows)
    first = carry is None
    z_spec = pl.BlockSpec((tile_m, columns), lambda m, n: (m, 0))
    g_spec = pl.BlockSpec((columns, columns), lambda m, n: (0, 0))
    return pl.pallas_call(
        lambda *refs: product_kernel(scale, first, *refs),
        grid=(cols // tile_m, rows // tile_n),
        in_specs=[
            pl.BlockSpec((width, tile_n), lambda m, n: (0, n)),
            pl.BlockSpec((tile_n, columns), lambda m, n: (n, 0)),
            pl.BlockSpec((tile_m, 4 * width), lambda m, n: (m, 0)),
        ]
        + ([] if first else [z_spec, g_spec]),
        out_specs=[z_spec, g_spec],
        out_shape=[
            jax.ShapeDtypeStruct((cols, columns), F32),
            jax.ShapeDtypeStruct((columns, columns), F32),
        ],
        name="kernel_times_sketch",
    )(x_t, s, y4, *(() if first else carry))


def final_kernel(index, g_ref, z_ref, s_ref, basis_ref, projected_ref, w):
    w[...] = inverse_factor(g_ref[...])
    own_r, own_c = projected_ref.shape[0], basis_ref.shape[0]
    wc = jnp.concatenate(split(w[pl.ds(pl.multiple_of(index[1] * own_c, own_c), own_c), :]), axis=0)
    both = mm(wc, s_ref[...], NT)
    basis_ref[...] = both[:own_c] + both[own_c:]
    wr = split(w[pl.ds(pl.multiple_of(index[0] * own_r, own_r), own_r), :])
    wr2 = jnp.concatenate(wr, axis=0)
    tile = 512
    for j in range(z_ref.shape[0] // tile):
        high, low = split(z_ref[tile * j : tile * (j + 1), :])
        both = mm(wr2, high, NT)
        projected_ref[:, tile * j : tile * (j + 1)] = (
            both[:own_r] + both[own_r:] + mm(wr[0], low, NT)
        )


def final_call(index, gram, z, s, own_r, own_c):
    columns = gram.shape[0]
    vmem = pl.BlockSpec(memory_space=pltpu.VMEM)
    return pl.pallas_call(
        final_kernel,
        in_specs=[pl.BlockSpec(memory_space=pltpu.SMEM), vmem, vmem, vmem],
        out_specs=[vmem, vmem],
        out_shape=[
            jax.ShapeDtypeStruct((own_c, s.shape[0]), F32),
            jax.ShapeDtypeStruct((own_r, z.shape[0]), F32),
        ],
        scratch_shapes=[pltpu.VMEM((columns, columns), F32)],
        name="factor_and_project",
    )(index, gram, z, s)


def swap(a, axis, bits):
    return lax.ppermute(a, axis, [(i, i ^ bits) for i in range(lax.axis_size(axis))])


def spread_chips(piece, axis):
    chips_z = lax.axis_size("rows") // 2
    chips_y = lax.axis_size("cols") // 2
    own = jnp.concatenate([piece] + [swap(piece, "rows", 2 * d) for d in range(1, chips_z)], axis)
    near_x = swap(own, "rows", 1)
    near_y = [swap(own, "cols", 2 * d) for d in range(1, chips_y)]
    half = own.shape[axis] // 2
    cut = lambda a, i: lax.slice_in_dim(a, i * half, (i + 1) * half, axis=axis)
    far = [
        jnp.concatenate([swap(cut(a, 0), "rows", 1), swap(cut(near_x, 1), "cols", 2 * d + 2)], axis)
        for d, a in enumerate(near_y)
    ]
    return own, [near_x] + near_y, far


def local(row_features, col_features, test_block):
    cols = lax.axis_size("cols")
    rows = lax.axis_size("rows")
    chips_y = cols // 2
    ir, ic = lax.axis_index("rows"), lax.axis_index("cols")
    core, iy = ic % 2, ic // 2
    height, width = row_features.shape
    scale = 1.0 / math.sqrt(width)
    columns = test_block.shape[1]
    half = height // 2
    quarter = half // chips_y

    x_t, y_t = row_features.T, col_features.T
    x_own = lax.dynamic_slice_in_dim(x_t, core * half + iy * quarter, quarter, 1)
    both = lambda a, axis: jnp.concatenate([a, swap(a, "cols", 1)], axis)
    x_a, x_b, x_c = spread_chips(x_own, 1)
    x_b, x_c = jnp.concatenate(x_b, 1), jnp.concatenate(x_c, 1)

    partial, y4 = sketch_call(x_t, y_t, test_block, scale)
    mine = lax.dynamic_slice_in_dim(partial, core * half, half, 0)
    given = lax.dynamic_slice_in_dim(partial, (1 - core) * half, half, 0)
    mine = mine + swap(given, "cols", 1)
    s_own = lax.dynamic_slice_in_dim(mine, iy * quarter, quarter, 0)
    for d in range(1, chips_y):
        given = lax.dynamic_slice_in_dim(mine, (iy ^ d) * quarter, quarter, 0)
        s_own = s_own + swap(given, "cols", 2 * d)
    s_own = s_own.astype(BF16)

    s_a, s_b, s_c = spread_chips(s_own, 0)
    pieces = [s_own] + [a[:quarter] for a in s_b[1:]]
    pieces = jnp.concatenate(pieces, 0)
    pieces = [pieces, swap(pieces, "cols", 1)]
    s_block = jnp.zeros((height, columns), BF16)
    for k in range(2):
        for d in range(chips_y):
            s_block = lax.dynamic_update_slice_in_dim(
                s_block,
                pieces[k][d * quarter : (d + 1) * quarter],
                (core ^ k) * half + (iy ^ d) * quarter,
                0,
            )
    s_b, s_c = jnp.concatenate(s_b, 0), jnp.concatenate(s_c, 0)

    carry = product_call(both(x_a, 1), both(s_a, 0), y4, scale)
    carry = product_call(both(x_b, 1), both(s_b, 0), y4, scale, carry)
    z, gram = product_call(both(x_c, 1), both(s_c, 0), y4, scale, carry)

    index = jnp.stack([ir, ic]).astype(jnp.int32)
    basis_t, projected = final_call(index, gram, z, s_block, columns // rows, columns // cols)
    return (basis_t.T, projected)


def solution(mesh):
    in_specs = (P("rows", None), P("cols", None), P("cols", None))
    out_specs = (P("rows", "cols"), P("rows", "cols"))
    return jax.shard_map(local, mesh=mesh, in_specs=in_specs, out_specs=out_specs, check_vma=False)
```

```python
import math

import jax
import jax.numpy as jnp
from jax import lax
from jax.experimental import pallas as pl
from jax.experimental.pallas import tpu as pltpu
from jax.sharding import PartitionSpec as P

F32 = jnp.float32
BF16 = jnp.bfloat16
NN = ((1,), (0,))
NT = ((1,), (1,))
TN = ((0,), (0,))


def mm(a, b, dims, precision=None):
    return lax.dot_general(
        a, b, (dims, ((), ())), precision=precision, preferred_element_type=F32
    )


def split(a):
    high = a.astype(BF16)
    return high, (a - high.astype(F32)).astype(BF16)


def cube(inner):
    shifted = inner + 1.0
    return (shifted * shifted * shifted).astype(BF16)


def factor_inverse(rows, n):
    blocks = n // 8
    lane = lax.broadcasted_iota(jnp.int32, (8, n), 1)
    sub = lax.broadcasted_iota(jnp.int32, (8, n), 0)
    rows = list(rows)
    done = []

    def row_of(a, t):
        return jnp.broadcast_to(a[t : t + 1, :], (8, n))

    for g in range(blocks):
        first = 8 * g
        inside = (lane >= first) & (lane < first + 8)
        pivot = jnp.where(inside, jnp.where(lane == sub + first, 1.0, 0.0), rows[g])
        column = [
            [jnp.broadcast_to(rows[v][:, first + k : first + k + 1], (8, n)) for k in range(8)]
            for v in range(g, blocks)
        ]
        factor = [[None] * 8 for _ in range(g, blocks)]
        diagonal = jnp.zeros((8, n), F32)
        for t in range(8):
            d = row_of(column[0][t], t)
            diagonal = jnp.where(sub == t, d, diagonal)
            r = 1.0 / d
            own = jnp.where(sub > t, column[0][t] * r, 0.0)
            for v in range(1, blocks - g):
                factor[v][t] = column[v][t] * r
            for k in range(t + 1, 8):
                e = row_of(column[0][k], t)
                column[0][k] = column[0][k] - own * e
                for v in range(1, blocks - g):
                    column[v][k] = column[v][k] - factor[v][t] * e
            pivot = pivot - own * row_of(pivot, t)
        pivots = [row_of(pivot, t) for t in range(8)]
        for v in range(1, blocks - g):
            m = jnp.where(inside, 0.0, rows[g + v])
            for t in range(8):
                m = m - factor[v][t] * pivots[t]
            rows[g + v] = m
        done.append(jnp.where(lane <= sub + first, pivot, 0.0) * lax.rsqrt(diagonal))
    return jnp.concatenate(done, axis=0)


def inverse_factor(gram, base=128):
    n = gram.shape[0]
    if n <= base:
        return factor_inverse([gram[8 * i : 8 * i + 8, :] for i in range(n // 8)], n)
    k = n // 2
    high = lax.Precision.HIGHEST
    w11 = inverse_factor(gram[:k, :k], base)
    l21 = mm(gram[k:, :k], w11, NT, high)
    w22 = inverse_factor(gram[k:, k:] - mm(l21, l21, NT, high), base)
    w21 = -mm(w22, mm(l21, w11, NN, high), NN, high)
    top = jnp.concatenate([w11, jnp.zeros((k, n - k), F32)], axis=1)
    return jnp.concatenate([top, jnp.concatenate([w21, w22], axis=1)], axis=0)


def sketch_kernel(scale, x_ref, y_ref, t_ref, mine_ref, given_ref, pairs_ref, x4, total):
    step = pl.program_id(0)

    @pl.when(step == 0)
    def _():
        pairs = jnp.concatenate(split(x_ref[...] * scale), axis=0).T
        x4[...] = jnp.concatenate([pairs, pairs], axis=1)
        pairs_ref[...] = pairs

    high, low = split(y_ref[...])
    y4 = jnp.concatenate([high, high, low, low], axis=0)
    part = mm(cube(mm(x4[...], y4, NN)), t_ref[...], NN)

    @pl.when(step == 0)
    def _():
        total[...] = part

    @pl.when(step > 0)
    def _():
        total[...] += part

    @pl.when(step == pl.num_programs(0) - 1)
    def _():
        half = mine_ref.shape[0]
        core = lax.axis_index("cols") % 2
        mine_ref[...] = total[pl.ds(pl.multiple_of(core * half, half), half), :]
        given_ref[...] = total[pl.ds(pl.multiple_of((1 - core) * half, half), half), :]


def sketch_call(x_t, y_t, test, scale):
    width, rows = x_t.shape
    cols, columns = test.shape
    tile = 1024
    whole = lambda shape: pl.BlockSpec(shape, lambda j: (0, 0))
    return pl.pallas_call(
        lambda *refs: sketch_kernel(scale, *refs),
        grid=(cols // tile,),
        in_specs=[
            whole((width, rows)),
            pl.BlockSpec((width, tile), lambda j: (0, j)),
            pl.BlockSpec((tile, columns), lambda j: (j, 0)),
        ],
        out_specs=[
            whole((rows // 2, columns)),
            whole((rows // 2, columns)),
            whole((rows, 2 * width)),
        ],
        out_shape=[
            jax.ShapeDtypeStruct((rows // 2, columns), F32),
            jax.ShapeDtypeStruct((rows // 2, columns), F32),
            jax.ShapeDtypeStruct((rows, 2 * width), BF16),
        ],
        scratch_shapes=[pltpu.VMEM((rows, 4 * width), BF16), pltpu.VMEM((rows, columns), F32)],
        name="sketch_tile",
    )(x_t, y_t, test)


def product_kernel(columns, count, first, *refs):
    pieces, refs = refs[:count], refs[count:]
    y_ref, refs = refs[0], refs[1:]
    (z_in, g_in), (z_ref, g_ref) = ((None, None), refs) if first else (refs[:2], refs[2:])
    m = pl.program_id(0)
    tile = z_ref.shape[0]
    start = (lax.axis_index("rows") % 2) * (y_ref.shape[1] // 2) + m * tile
    high, low = split(y_ref[:, pl.ds(pl.multiple_of(start, tile), tile)])
    y4 = jnp.concatenate([high, high, low, low], axis=0).T
    total = None if first else z_in[...]
    for piece in pieces:
        pairs = piece[:, columns:]
        k = cube(mm(y4, jnp.concatenate([pairs, pairs], axis=1), NT))
        part = mm(k, piece[:, :columns], NN)
        total = part if total is None else total + part
    z_ref[...] = total

    @pl.when(m == 0)
    def _():
        gram = None if first else g_in[...]
        for piece in pieces:
            s = piece[:, :columns]
            part = mm(s, s, TN)
            gram = part if gram is None else gram + part
        g_ref[...] = gram


def product_call(pieces, y_t, columns, carry=None):
    cols = y_t.shape[1] // 2
    tile = 1024
    first = carry is None
    whole = lambda shape: pl.BlockSpec(shape, lambda m: (0, 0))
    z_spec = pl.BlockSpec((tile, columns), lambda m: (m, 0))
    g_spec = whole((columns, columns))
    return pl.pallas_call(
        lambda *refs: product_kernel(columns, len(pieces), first, *refs),
        grid=(cols // tile,),
        in_specs=[whole(a.shape) for a in pieces]
        + [whole(y_t.shape)]
        + ([] if first else [z_spec, g_spec]),
        out_specs=[z_spec, g_spec],
        out_shape=[
            jax.ShapeDtypeStruct((cols, columns), F32),
            jax.ShapeDtypeStruct((columns, columns), F32),
        ],
        name="kernel_times_sketch",
    )(*pieces, y_t, *(() if first else carry))


def final_kernel(places, g_ref, z_ref, *refs):
    pieces, (basis_ref, projected_ref, given_ref, w, s) = refs[: len(places)], refs[len(places) :]
    quarter = pieces[0].shape[0]
    for place, piece in zip(places, pieces):
        s[pl.ds(pl.multiple_of(place() * quarter, quarter), quarter), :] = piece[...]
    w[...] = inverse_factor(g_ref[...])
    own_r, own_c = projected_ref.shape[0], basis_ref.shape[0]
    ir, ic = lax.axis_index("rows"), lax.axis_index("cols")

    def rows_of(i, n):
        return split(w[pl.ds(pl.multiple_of(i * n, n), n), :])

    both = mm(jnp.concatenate(rows_of(ic, own_c), axis=0), s[...], NT)
    basis_ref[...] = both[:own_c] + both[own_c:]
    mine, given = rows_of(ir, own_r), rows_of(ir ^ 1, own_r)
    tall = jnp.concatenate([mine[0], given[0], mine[1], given[1]], axis=0)
    cols = z_ref.shape[0]
    start = (ir % 2) * cols
    tile = 512
    for j in range(cols // tile):
        high, low = split(z_ref[tile * j : tile * (j + 1), :])
        both = mm(tall, high, NT)
        both = both[: 2 * own_r] + both[2 * own_r :] + mm(tall[: 2 * own_r], low, NT)
        there = pl.ds(pl.multiple_of(start + tile * j, tile), tile)
        projected_ref[:, there] = both[:own_r]
        given_ref[:, tile * j : tile * (j + 1)] = both[own_r:].astype(BF16)


def final_call(gram, z, pieces, places, quarter, own_r, own_c):
    columns = gram.shape[0]
    whole = lambda shape: pl.BlockSpec(shape, lambda i: (0, 0))
    height = quarter * len(pieces)
    cols = z.shape[0]
    return pl.pallas_call(
        lambda *refs: final_kernel(places, *refs),
        grid=(1,),
        in_specs=[whole(gram.shape), whole(z.shape)] + [whole((quarter, columns)) for _ in pieces],
        out_specs=[whole((own_c, height)), whole((own_r, 2 * cols)), whole((own_r, cols))],
        out_shape=[
            jax.ShapeDtypeStruct((own_c, height), F32),
            jax.ShapeDtypeStruct((own_r, 2 * cols), F32),
            jax.ShapeDtypeStruct((own_r, cols), BF16),
        ],
        scratch_shapes=[pltpu.VMEM((columns, columns), F32), pltpu.VMEM((height, columns), BF16)],
        name="factor_and_project",
    )(gram, z, *pieces)


def swap(a, axis, bits):
    return lax.ppermute(a, axis, [(i, i ^ bits) for i in range(lax.axis_size(axis))])


def local(row_features, col_features, test_block):
    cols = lax.axis_size("cols")
    rows = lax.axis_size("rows")
    chips_y, chips_z = cols // 2, rows // 2
    ir, ic = lax.axis_index("rows"), lax.axis_index("cols")
    core, iy = ic % 2, ic // 2
    height, width = row_features.shape
    scale = 1.0 / math.sqrt(width)
    columns = test_block.shape[1]
    half = height // 2
    quarter = half // chips_y

    x_t, y_t = row_features.T, col_features.T
    mine, given, pairs = sketch_call(x_t, y_t, test_block, scale)
    mine = mine + swap(given, "cols", 1)
    s_own = lax.dynamic_slice_in_dim(mine, iy * quarter, quarter, 0)
    for d in range(1, chips_y):
        given = lax.dynamic_slice_in_dim(mine, (iy ^ d) * quarter, quarter, 0)
        s_own = s_own + swap(given, "cols", 2 * d)
    pairs = lax.dynamic_slice_in_dim(pairs, core * half + iy * quarter, quarter, 0)
    piece = jnp.concatenate([s_own.astype(BF16), pairs], axis=1)

    own = jnp.concatenate([piece] + [swap(piece, "rows", 2 * d) for d in range(1, chips_z)], 0)
    near_x = swap(own, "rows", 1)
    near_y = [swap(own, "cols", 2 * d) for d in range(1, chips_y)]
    own_core = swap(own, "cols", 1)
    carry = product_call([own, own_core], y_t, columns)
    cut = own.shape[0] // 2
    far = []
    for d in range(1, chips_y):
        far += [swap(near_y[d - 1][:cut], "rows", 1), swap(near_x[cut:], "cols", 2 * d)]
    near = [near_x] + near_y
    near_core = [swap(a, "cols", 1) for a in near]
    carry = product_call(near + near_core, y_t, columns, carry)
    far_core = [swap(a, "cols", 1) for a in far]
    z, gram = product_call(far + far_core, y_t, columns, carry)

    pieces, places = [], []
    for k, group in enumerate(([own] + near_y, [own_core] + near_core[1:])):
        for d, a in enumerate(group):
            pieces.append(a)

            def place(k=k, d=d):
                c = lax.axis_index("cols")
                return ((c % 2) ^ k) * chips_y + ((c // 2) ^ d)

            places.append(place)
    basis_t, projected, given = final_call(
        gram, z, pieces, places, quarter, columns // rows, columns // cols
    )
    there = swap(given, "rows", 1).astype(F32)
    projected = lax.dynamic_update_slice_in_dim(
        projected, there, (1 - ir % 2) * there.shape[1], 1
    )
    return (basis_t.T, projected)


def solution(mesh):
    in_specs = (P("rows", None), P("cols", None), P("cols", None))
    out_specs = (P("rows", "cols"), P("rows", "cols"))
    return jax.shard_map(local, mesh=mesh, in_specs=in_specs, out_specs=out_specs, check_vma=False)
```

```python
import math

import jax
import jax.numpy as jnp
from jax import lax
from jax.experimental import pallas as pl
from jax.experimental.pallas import tpu as pltpu
from jax.sharding import PartitionSpec as P


F32 = jnp.float32
BF16 = jnp.bfloat16
NN = ((1,), (0,))
NT = ((1,), (1,))
TN = ((0,), (0,))


def mm(a, b, dims, precision=None):
    return lax.dot_general(
        a, b, (dims, ((), ())), precision=precision, preferred_element_type=F32
    )


def split(a):
    high = a.astype(BF16)
    return high, (a - high.astype(F32)).astype(BF16)


def cube(inner):
    shifted = inner + 1.0
    return (shifted * shifted * shifted).astype(BF16)


def factor_inverse(rows, n):
    blocks = n // 8
    lane = lax.broadcasted_iota(jnp.int32, (8, n), 1)
    sub = lax.broadcasted_iota(jnp.int32, (8, n), 0)
    rows = list(rows)
    done = []

    def row_of(a, t):
        return jnp.broadcast_to(a[t : t + 1, :], (8, n))

    for g in range(blocks):
        first = 8 * g
        inside = (lane >= first) & (lane < first + 8)
        pivot = jnp.where(inside, jnp.where(lane == sub + first, 1.0, 0.0), rows[g])
        column = [
            [jnp.broadcast_to(rows[v][:, first + k : first + k + 1], (8, n)) for k in range(8)]
            for v in range(g, blocks)
        ]
        factor = [[None] * 8 for _ in range(g, blocks)]
        diagonal = jnp.zeros((8, n), F32)
        for t in range(8):
            d = row_of(column[0][t], t)
            diagonal = jnp.where(sub == t, d, diagonal)
            r = 1.0 / d
            own = jnp.where(sub > t, column[0][t] * r, 0.0)
            for v in range(1, blocks - g):
                factor[v][t] = column[v][t] * r
            for k in range(t + 1, 8):
                e = row_of(column[0][k], t)
                column[0][k] = column[0][k] - own * e
                for v in range(1, blocks - g):
                    column[v][k] = column[v][k] - factor[v][t] * e
            pivot = pivot - own * row_of(pivot, t)
        pivots = [row_of(pivot, t) for t in range(8)]
        for v in range(1, blocks - g):
            m = jnp.where(inside, 0.0, rows[g + v])
            for t in range(8):
                m = m - factor[v][t] * pivots[t]
            rows[g + v] = m
        done.append(jnp.where(lane <= sub + first, pivot, 0.0) * lax.rsqrt(diagonal))
    return jnp.concatenate(done, axis=0)


def inverse_factor(gram, base=128):
    n = gram.shape[0]
    if n <= base:
        return factor_inverse([gram[8 * i : 8 * i + 8, :] for i in range(n // 8)], n)
    k = n // 2
    high = lax.Precision.HIGHEST
    w11 = inverse_factor(gram[:k, :k], base)
    l21 = mm(gram[k:, :k], w11, NT, high)
    w22 = inverse_factor(gram[k:, k:] - mm(l21, l21, NT, high), base)
    w21 = -mm(w22, mm(l21, w11, NN, high), NN, high)
    top = jnp.concatenate([w11, jnp.zeros((k, n - k), F32)], axis=1)
    return jnp.concatenate([top, jnp.concatenate([w21, w22], axis=1)], axis=0)


def sketch_kernel(scale, x_ref, y_ref, t_ref, mine_ref, given_ref, pairs_ref, x4, total):
    step = pl.program_id(0)

    @pl.when(step == 0)
    def _():
        pairs = jnp.concatenate(split(x_ref[...] * scale), axis=0).T
        x4[...] = jnp.concatenate([pairs, pairs], axis=1)
        pairs_ref[...] = pairs

    high, low = split(y_ref[...])
    y4 = jnp.concatenate([high, high, low, low], axis=0)
    part = mm(cube(mm(x4[...], y4, NN)), t_ref[...], NN)

    @pl.when(step == 0)
    def _():
        total[...] = part

    @pl.when(step > 0)
    def _():
        total[...] += part

    @pl.when(step == pl.num_programs(0) - 1)
    def _():
        half = mine_ref.shape[0]
        core = lax.axis_index("cols") % 2
        mine_ref[...] = total[pl.ds(pl.multiple_of(core * half, half), half), :]
        given_ref[...] = total[pl.ds(pl.multiple_of((1 - core) * half, half), half), :]


def sketch_call(x_t, y_t, test, scale):
    width, rows = x_t.shape
    cols, columns = test.shape
    tile = 1024
    whole = lambda shape: pl.BlockSpec(shape, lambda j: (0, 0))
    return pl.pallas_call(
        lambda *refs: sketch_kernel(scale, *refs),
        grid=(cols // tile,),
        in_specs=[
            whole((width, rows)),
            pl.BlockSpec((width, tile), lambda j: (0, j)),
            pl.BlockSpec((tile, columns), lambda j: (j, 0)),
        ],
        out_specs=[
            whole((rows // 2, columns)),
            whole((rows // 2, columns)),
            whole((rows, 2 * width)),
        ],
        out_shape=[
            jax.ShapeDtypeStruct((rows // 2, columns), F32),
            jax.ShapeDtypeStruct((rows // 2, columns), F32),
            jax.ShapeDtypeStruct((rows, 2 * width), BF16),
        ],
        scratch_shapes=[pltpu.VMEM((rows, 4 * width), BF16), pltpu.VMEM((rows, columns), F32)],
        name="sketch_tile",
    )(x_t, y_t, test)


def product_kernel(columns, count, first, *refs):
    pieces, refs = refs[:count], refs[count:]
    y_ref, refs = refs[0], refs[1:]
    (z_in, g_in), (z_ref, g_ref) = ((None, None), refs) if first else (refs[:2], refs[2:])
    m = pl.program_id(0)
    tile = z_ref.shape[0]
    start = (lax.axis_index("rows") % 2) * (y_ref.shape[1] // 2) + m * tile
    high, low = split(y_ref[:, pl.ds(pl.multiple_of(start, tile), tile)])
    y4 = jnp.concatenate([high, high, low, low], axis=0).T
    total = None if first else z_in[...]
    for piece in pieces:
        pairs = piece[:, columns:]
        k = cube(mm(y4, jnp.concatenate([pairs, pairs], axis=1), NT))
        part = mm(k, piece[:, :columns], NN)
        total = part if total is None else total + part
    z_ref[...] = total

    @pl.when(m == 0)
    def _():
        gram = None if first else g_in[...]
        for piece in pieces:
            s = piece[:, :columns]
            part = mm(s, s, TN)
            gram = part if gram is None else gram + part
        g_ref[...] = gram


def product_call(pieces, y_t, columns, carry=None):
    cols = y_t.shape[1] // 2
    tile = 1024
    first = carry is None
    whole = lambda shape: pl.BlockSpec(shape, lambda m: (0, 0))
    z_spec = pl.BlockSpec((tile, columns), lambda m: (m, 0))
    g_spec = whole((columns, columns))
    return pl.pallas_call(
        lambda *refs: product_kernel(columns, len(pieces), first, *refs),
        grid=(cols // tile,),
        in_specs=[whole(a.shape) for a in pieces]
        + [whole(y_t.shape)]
        + ([] if first else [z_spec, g_spec]),
        out_specs=[z_spec, g_spec],
        out_shape=[
            jax.ShapeDtypeStruct((cols, columns), F32),
            jax.ShapeDtypeStruct((columns, columns), F32),
        ],
        cost_estimate=pl.CostEstimate(
            flops=2 * cols * sum(a.shape[0] for a in pieces) * (columns + 4 * y_t.shape[0]),
            bytes_accessed=4 * (2 * cols * columns + y_t.size) + 2 * sum(a.size for a in pieces),
            transcendentals=0,
        ),
        name="kernel_times_sketch",
    )(*pieces, y_t, *(() if first else carry))


def final_kernel(places, g_ref, z_ref, *refs):
    pieces, (basis_ref, projected_ref, given_ref, w, s) = refs[: len(places)], refs[len(places) :]
    quarter = pieces[0].shape[0]
    for place, piece in zip(places, pieces):
        s[pl.ds(pl.multiple_of(place() * quarter, quarter), quarter), :] = piece[...]
    w[...] = inverse_factor(g_ref[...])
    own_r, own_c = projected_ref.shape[0], basis_ref.shape[0]
    ir, ic = lax.axis_index("rows"), lax.axis_index("cols")

    def rows_of(i, n):
        return split(w[pl.ds(pl.multiple_of(i * n, n), n), :])

    both = mm(jnp.concatenate(rows_of(ic, own_c), axis=0), s[...], NT)
    basis_ref[...] = both[:own_c] + both[own_c:]
    mine, given = rows_of(ir, own_r), rows_of(ir ^ 1, own_r)
    tall = jnp.concatenate([mine[0], given[0], mine[1], given[1]], axis=0)
    cols = z_ref.shape[0]
    start = (ir % 2) * cols
    tile = 512
    for j in range(cols // tile):
        high, low = split(z_ref[tile * j : tile * (j + 1), :])
        both = mm(tall, high, NT)
        both = both[: 2 * own_r] + both[2 * own_r :] + mm(tall[: 2 * own_r], low, NT)
        there = pl.ds(pl.multiple_of(start + tile * j, tile), tile)
        projected_ref[:, there] = both[:own_r]
        given_ref[:, tile * j : tile * (j + 1)] = both[own_r:].astype(BF16)


def final_call(gram, z, pieces, places, quarter, own_r, own_c):
    columns = gram.shape[0]
    whole = lambda shape: pl.BlockSpec(shape, lambda i: (0, 0))
    height = quarter * len(pieces)
    cols = z.shape[0]
    return pl.pallas_call(
        lambda *refs: final_kernel(places, *refs),
        grid=(1,),
        in_specs=[whole(gram.shape), whole(z.shape)] + [whole((quarter, columns)) for _ in pieces],
        out_specs=[whole((own_c, height)), whole((own_r, 2 * cols)), whole((own_r, cols))],
        out_shape=[
            jax.ShapeDtypeStruct((own_c, height), F32),
            jax.ShapeDtypeStruct((own_r, 2 * cols), F32),
            jax.ShapeDtypeStruct((own_r, cols), BF16),
        ],
        scratch_shapes=[pltpu.VMEM((columns, columns), F32), pltpu.VMEM((height, columns), BF16)],
        name="factor_and_project",
    )(gram, z, *pieces)


def swap(a, axis, bits):
    return lax.ppermute(a, axis, [(i, i ^ bits) for i in range(lax.axis_size(axis))])


def local(row_features, col_features, test_block):
    cols = lax.axis_size("cols")
    rows = lax.axis_size("rows")
    chips_y, chips_z = cols // 2, rows // 2
    ir, ic = lax.axis_index("rows"), lax.axis_index("cols")
    core, iy = ic % 2, ic // 2
    height, width = row_features.shape
    scale = 1.0 / math.sqrt(width)
    columns = test_block.shape[1]
    half = height // 2
    quarter = half // chips_y

    x_t, y_t = row_features.T, col_features.T
    mine, given, pairs = sketch_call(x_t, y_t, test_block, scale)
    mine = mine + swap(given, "cols", 1)
    s_own = lax.dynamic_slice_in_dim(mine, iy * quarter, quarter, 0)
    for d in range(1, chips_y):
        given = lax.dynamic_slice_in_dim(mine, (iy ^ d) * quarter, quarter, 0)
        s_own = s_own + swap(given, "cols", 2 * d)
    pairs = lax.dynamic_slice_in_dim(pairs, core * half + iy * quarter, quarter, 0)
    piece = jnp.concatenate([s_own.astype(BF16), pairs], axis=1)

    own = jnp.concatenate([piece] + [swap(piece, "rows", 2 * d) for d in range(1, chips_z)], 0)
    near_x = swap(own, "rows", 1)
    near_y = [swap(own, "cols", 2 * d) for d in range(1, chips_y)]
    own_core = swap(own, "cols", 1)
    carry = product_call([own, own_core], y_t, columns)
    cut = own.shape[0] // 2
    far = []
    for d in range(1, chips_y):
        far.append(swap(near_y[d - 1][:cut], "rows", 1))
        far.append(swap(near_x[cut:], "cols", 2 * d))
    near = [near_x] + near_y
    near_core = [swap(a, "cols", 1) for a in near]
    carry = product_call(near + near_core, y_t, columns, carry)
    far_core = [swap(a, "cols", 1) for a in far]
    z, gram = product_call(far + far_core, y_t, columns, carry)

    pieces, places = [], []
    for k, group in enumerate(([own] + near_y, [own_core] + near_core[1:])):
        for d, a in enumerate(group):
            pieces.append(a)

            def place(k=k, d=d):
                c = lax.axis_index("cols")
                return ((c % 2) ^ k) * chips_y + ((c // 2) ^ d)

            places.append(place)
    basis_t, projected, given = final_call(
        gram, z, pieces, places, quarter, columns // rows, columns // cols
    )
    there = swap(given, "rows", 1).astype(F32)
    projected = lax.dynamic_update_slice_in_dim(
        projected, there, (1 - ir % 2) * there.shape[1], 1
    )
    return (basis_t.T, projected)


def solution(mesh):
    in_specs = (P("rows", None), P("cols", None), P("cols", None))
    out_specs = (P("rows", "cols"), P("rows", "cols"))
    return jax.shard_map(local, mesh=mesh, in_specs=in_specs, out_specs=out_specs, check_vma=False)
```

```python
import math

import jax
import jax.numpy as jnp
from jax import lax
from jax.experimental import pallas as pl
from jax.experimental.pallas import tpu as pltpu
from jax.sharding import PartitionSpec as P


F32 = jnp.float32
BF16 = jnp.bfloat16
NN = ((1,), (0,))
NT = ((1,), (1,))
TN = ((0,), (0,))


def mm(a, b, dims, precision=None):
    return lax.dot_general(
        a, b, (dims, ((), ())), precision=precision, preferred_element_type=F32
    )


def split(a):
    high = a.astype(BF16)
    return high, (a - high.astype(F32)).astype(BF16)


def cube(inner):
    shifted = inner + 1.0
    return (shifted * shifted * shifted).astype(BF16)


def three(a):
    high = a.astype(BF16).astype(F32)
    rest = a - high
    middle = rest.astype(BF16).astype(F32)
    return high, middle, rest - middle


def factor_inverse(rows, n, jobs):
    blocks = n // 8
    lane = lax.broadcasted_iota(jnp.int32, (8, n), 1)
    sub = lax.broadcasted_iota(jnp.int32, (8, n), 0)
    rows = list(rows)
    done = []

    def row_of(a, t):
        return jnp.broadcast_to(a[t : t + 1, :], (8, n))

    for g in range(blocks):
        first = 8 * g
        inside = (lane >= first) & (lane < first + 8)
        pivot = jnp.where(inside, jnp.where(lane == sub + first, 1.0, 0.0), rows[g])
        near = min(g + 2, blocks) - g
        column = [
            [jnp.broadcast_to(rows[g + v][:, first + k : first + k + 1], (8, n)) for k in range(8)]
            for v in range(near)
        ]
        factor = [None] * 8
        diagonal = jnp.zeros((8, n), F32)
        if jobs:
            jobs.pop(0)()
        for t in range(8):
            diagonal = jnp.where(sub == t, column[0][t], diagonal)
            r = row_of(1.0 / column[0][t], t)
            own = jnp.where(sub > t, column[0][t] * r, 0.0)
            if near > 1:
                factor[t] = column[1][t] * r
            for k in range(t + 1, 8):
                e = row_of(column[0][k], t)
                column[0][k] = column[0][k] - own * e
                if near > 1:
                    column[1][k] = column[1][k] - factor[t] * e
            pivot = pivot - own * row_of(pivot, t)
        if g + 2 < blocks:
            a1, a2, a3 = three(pivot * (1.0 / diagonal))
            b1, b2, b3 = three(pivot)
            left = jnp.concatenate([a1, a1, a2, a2, a1, a3], axis=0).astype(BF16)
            right = jnp.concatenate([b1, b2, b1, b2, b3, b1], axis=0).astype(BF16)
            update = mm(left, right, TN)
            for v in range(g + 2, blocks):
                rows[v] = jnp.where(inside, 0.0, rows[v]) - update[8 * v : 8 * v + 8, :]
        if near > 1:
            m = jnp.where(inside, 0.0, rows[g + 1])
            for t in range(8):
                m = m - factor[t] * row_of(pivot, t)
            rows[g + 1] = m
        done.append(jnp.where(lane <= sub + first, pivot, 0.0) * lax.rsqrt(diagonal))
    return jnp.concatenate(done, axis=0)


def inverse_factor(gram, jobs, base=128):
    n = gram.shape[0]
    if n <= base:
        return factor_inverse([gram[8 * i : 8 * i + 8, :] for i in range(n // 8)], n, jobs)
    k = n // 2
    high = lax.Precision.HIGHEST
    w11 = inverse_factor(gram[:k, :k], jobs, base)
    l21 = mm(gram[k:, :k], w11, NT, high)
    w22 = inverse_factor(gram[k:, k:] - mm(l21, l21, NT, high), jobs, base)
    w21 = -mm(w22, mm(l21, w11, NN, high), NN, high)
    top = jnp.concatenate([w11, jnp.zeros((k, n - k), F32)], axis=1)
    return jnp.concatenate([top, jnp.concatenate([w21, w22], axis=1)], axis=0)


def sketch_kernel(scale, x_ref, y_ref, t_ref, mine_ref, given_ref, pairs_ref, x4, total):
    step = pl.program_id(0)

    @pl.when(step == 0)
    def _():
        pairs = jnp.concatenate(split(x_ref[...] * scale), axis=0).T
        x4[...] = jnp.concatenate([pairs, pairs], axis=1)
        pairs_ref[...] = pairs

    high, low = split(y_ref[...])
    y4 = jnp.concatenate([high, high, low, low], axis=0)
    part = mm(cube(mm(x4[...], y4, NN)), t_ref[...], NN)

    @pl.when(step == 0)
    def _():
        total[...] = part

    @pl.when(step > 0)
    def _():
        total[...] += part

    @pl.when(step == pl.num_programs(0) - 1)
    def _():
        half = mine_ref.shape[0]
        core = lax.axis_index("cols") % 2
        mine_ref[...] = total[pl.ds(pl.multiple_of(core * half, half), half), :]
        given_ref[...] = total[pl.ds(pl.multiple_of((1 - core) * half, half), half), :]


def sketch_call(x_t, y_t, test, scale):
    width, rows = x_t.shape
    cols, columns = test.shape
    tile = 1024
    whole = lambda shape: pl.BlockSpec(shape, lambda j: (0, 0))
    return pl.pallas_call(
        lambda *refs: sketch_kernel(scale, *refs),
        grid=(cols // tile,),
        in_specs=[
            whole((width, rows)),
            pl.BlockSpec((width, tile), lambda j: (0, j)),
            pl.BlockSpec((tile, columns), lambda j: (j, 0)),
        ],
        out_specs=[
            whole((rows // 2, columns)),
            whole((rows // 2, columns)),
            whole((rows, 2 * width)),
        ],
        out_shape=[
            jax.ShapeDtypeStruct((rows // 2, columns), F32),
            jax.ShapeDtypeStruct((rows // 2, columns), F32),
            jax.ShapeDtypeStruct((rows, 2 * width), BF16),
        ],
        scratch_shapes=[pltpu.VMEM((rows, 4 * width), BF16), pltpu.VMEM((rows, columns), F32)],
        name="sketch_tile",
    )(x_t, y_t, test)


def columns_kernel(y_ref, y4_ref):
    cols = y4_ref.shape[0]
    start = (lax.axis_index("rows") % 2) * cols
    high, low = split(y_ref[:, pl.ds(pl.multiple_of(start, cols), cols)])
    y4_ref[...] = jnp.concatenate([high, high, low, low], axis=0).T


def columns_call(y_t):
    width, cols = y_t.shape
    return pl.pallas_call(
        columns_kernel,
        out_shape=jax.ShapeDtypeStruct((cols // 2, 4 * width), BF16),
        cost_estimate=pl.CostEstimate(
            flops=0, bytes_accessed=4 * y_t.size + 4 * width * cols, transcendentals=0
        ),
        name="column_pieces",
    )(y_t)


def rows_of_kernel(y4, piece, columns):
    pairs = piece[:, columns:]
    k = cube(mm(y4, jnp.concatenate([pairs, pairs], axis=1), NT))
    return mm(k, piece[:, :columns], NN)


def gram_of(pieces, columns, total=None):
    for piece in pieces:
        s = piece[:, :columns]
        part = mm(s, s, TN)
        total = part if total is None else total + part
    return total


def product_kernel(columns, count, first, *refs):
    pieces, refs = refs[:count], refs[count:]
    y4_ref, refs = refs[0], refs[1:]
    (z_in, g_in), (z_ref, g_ref) = ((None, None), refs) if first else (refs[:2], refs[2:])
    sub = 256
    for i in range(z_ref.shape[0] // sub):
        there = slice(i * sub, (i + 1) * sub)
        total = None if first else z_in[there, :]
        for piece in pieces:
            part = rows_of_kernel(y4_ref[there, :], piece, columns)
            total = part if total is None else total + part
        z_ref[there, :] = total

    @pl.when(pl.program_id(0) == 0)
    def _():
        g_ref[...] = gram_of(pieces, columns, None if first else g_in[...])


def product_call(pieces, y4, columns, carry=None):
    cols, depth = y4.shape
    tile = 1024
    first = carry is None
    whole = lambda shape: pl.BlockSpec(shape, lambda m: (0, 0))
    z_spec = pl.BlockSpec((tile, columns), lambda m: (m, 0))
    g_spec = whole((columns, columns))
    return pl.pallas_call(
        lambda *refs: product_kernel(columns, len(pieces), first, *refs),
        grid=(cols // tile,),
        in_specs=[whole(a.shape) for a in pieces]
        + [pl.BlockSpec((tile, depth), lambda m: (m, 0))]
        + ([] if first else [z_spec, g_spec]),
        out_specs=[z_spec, g_spec],
        out_shape=[
            jax.ShapeDtypeStruct((cols, columns), F32),
            jax.ShapeDtypeStruct((columns, columns), F32),
        ],
        cost_estimate=pl.CostEstimate(
            flops=2 * cols * sum(a.shape[0] for a in pieces) * (columns + depth),
            bytes_accessed=8 * cols * columns + 2 * y4.size + 2 * sum(a.size for a in pieces),
            transcendentals=0,
        ),
        name="kernel_times_sketch",
    )(*pieces, y4, *(() if first else carry))


def final_kernel(places, count, *refs):
    late, refs = refs[:count], refs[count:]
    (y4_ref, g_ref, z_hbm), refs = refs[:3], refs[3:]
    pieces, refs = refs[: len(places)], refs[len(places) :]
    basis_ref, projected_ref, given_ref, w, s, z, arrived = refs
    columns = g_ref.shape[0]
    cols = z.shape[0]
    copy = pltpu.make_async_copy(z_hbm, z, arrived)
    copy.start()
    quarter = pieces[0].shape[0]
    for place, piece in zip(places, pieces):
        s[pl.ds(pl.multiple_of(place() * quarter, quarter), quarter), :] = piece[...]
    gram = gram_of(late, columns, g_ref[...])
    copy.wait()

    sub = 256
    work = [(i, piece) for i in range(cols // sub) for piece in late]
    slots = columns // 8

    def job(part):
        def run():
            for i, piece in part:
                there = slice(i * sub, (i + 1) * sub)
                z[there, :] += rows_of_kernel(y4_ref[there, :], piece, columns)

        return run

    bounds = [len(work) * i // slots for i in range(slots + 1)]
    jobs = [job(work[i:j]) for i, j in zip(bounds, bounds[1:])]
    w[...] = inverse_factor(gram, jobs)

    own_r, own_c = projected_ref.shape[0], basis_ref.shape[0]
    ir, ic = lax.axis_index("rows"), lax.axis_index("cols")

    def rows_of(i, n):
        return split(w[pl.ds(pl.multiple_of(i * n, n), n), :])

    mine, given = rows_of(ir, own_r), rows_of(ir ^ 1, own_r)
    tall = jnp.concatenate([mine[0], given[0], mine[1], given[1]], axis=0)
    start = (ir % 2) * cols
    tile = 512
    for j in range(cols // tile):
        high, low = split(z[tile * j : tile * (j + 1), :])
        both = mm(tall, high, NT)
        both = both[: 2 * own_r] + both[2 * own_r :] + mm(tall[: 2 * own_r], low, NT)
        there = pl.ds(pl.multiple_of(start + tile * j, tile), tile)
        projected_ref[:, there] = both[:own_r]
        given_ref[:, tile * j : tile * (j + 1)] = both[own_r:].astype(BF16)
    both = mm(jnp.concatenate(rows_of(ic, own_c), axis=0), s[...], NT)
    basis_ref[...] = both[:own_c] + both[own_c:]


def final_call(late, y4, gram, z, pieces, places, quarter, own_r, own_c):
    columns = gram.shape[0]
    whole = lambda shape: pl.BlockSpec(shape, lambda i: (0, 0))
    height = quarter * len(pieces)
    cols = z.shape[0]
    return pl.pallas_call(
        lambda *refs: final_kernel(places, len(late), *refs),
        grid=(1,),
        in_specs=[whole(a.shape) for a in late]
        + [whole(y4.shape), whole(gram.shape), pl.BlockSpec(memory_space=pl.ANY)]
        + [whole((quarter, columns)) for _ in pieces],
        out_specs=[whole((own_c, height)), whole((own_r, 2 * cols)), whole((own_r, cols))],
        out_shape=[
            jax.ShapeDtypeStruct((own_c, height), F32),
            jax.ShapeDtypeStruct((own_r, 2 * cols), F32),
            jax.ShapeDtypeStruct((own_r, cols), BF16),
        ],
        scratch_shapes=[
            pltpu.VMEM((columns, columns), F32),
            pltpu.VMEM((height, columns), BF16),
            pltpu.VMEM((cols, columns), F32),
            pltpu.SemaphoreType.DMA,
        ],
        name="factor_and_project",
    )(*late, y4, gram, z, *pieces)


def swap(a, axis, bits):
    return lax.ppermute(a, axis, [(i, i ^ bits) for i in range(lax.axis_size(axis))])


def local(row_features, col_features, test_block):
    cols = lax.axis_size("cols")
    rows = lax.axis_size("rows")
    chips_y, chips_z = cols // 2, rows // 2
    ir, ic = lax.axis_index("rows"), lax.axis_index("cols")
    core, iy = ic % 2, ic // 2
    height, width = row_features.shape
    scale = 1.0 / math.sqrt(width)
    columns = test_block.shape[1]
    half = height // 2
    quarter = half // chips_y

    x_t, y_t = row_features.T, col_features.T
    mine, given, pairs = sketch_call(x_t, y_t, test_block, scale)
    y4 = columns_call(y_t)
    mine = mine + swap(given, "cols", 1)
    s_own = lax.dynamic_slice_in_dim(mine, iy * quarter, quarter, 0)
    for d in range(1, chips_y):
        given = lax.dynamic_slice_in_dim(mine, (iy ^ d) * quarter, quarter, 0)
        s_own = s_own + swap(given, "cols", 2 * d)
    pairs = lax.dynamic_slice_in_dim(pairs, core * half + iy * quarter, quarter, 0)
    piece = jnp.concatenate([s_own.astype(BF16), pairs], axis=1)

    own = jnp.concatenate([piece] + [swap(piece, "rows", 2 * d) for d in range(1, chips_z)], 0)
    near_x = swap(own, "rows", 1)
    near_y = [swap(own, "cols", 2 * d) for d in range(1, chips_y)]
    own_core = swap(own, "cols", 1)
    carry = product_call([own, own_core], y4, columns)
    cut = own.shape[0] // 2
    far = []
    for d in range(1, chips_y):
        far.append(swap(near_y[d - 1][:cut], "rows", 1))
        far.append(swap(near_x[cut:], "cols", 2 * d))
    near = [near_x] + near_y
    near_core = [swap(a, "cols", 1) for a in near]
    z, gram = product_call(near, y4, columns, carry)
    late = near_core + far + [swap(a, "cols", 1) for a in far]

    pieces, places = [], []
    for k, group in enumerate(([own] + near_y, [own_core] + near_core[1:])):
        for d, a in enumerate(group):
            pieces.append(a)

            def place(k=k, d=d):
                c = lax.axis_index("cols")
                return ((c % 2) ^ k) * chips_y + ((c // 2) ^ d)

            places.append(place)
    basis_t, projected, given = final_call(
        late, y4, gram, z, pieces, places, quarter, columns // rows, columns // cols
    )
    there = swap(given, "rows", 1).astype(F32)
    projected = lax.dynamic_update_slice_in_dim(
        projected, there, (1 - ir % 2) * there.shape[1], 1
    )
    return (basis_t.T, projected)


def solution(mesh):
    in_specs = (P("rows", None), P("cols", None), P("cols", None))
    out_specs = (P("rows", "cols"), P("rows", "cols"))
    return jax.shard_map(local, mesh=mesh, in_specs=in_specs, out_specs=out_specs, check_vma=False)
```

```python
import math

import jax
import jax.numpy as jnp
from jax import lax
from jax.experimental import pallas as pl
from jax.experimental.pallas import tpu as pltpu
from jax.sharding import PartitionSpec as P


F32 = jnp.float32
BF16 = jnp.bfloat16
NN = ((1,), (0,))
NT = ((1,), (1,))
TN = ((0,), (0,))


def mm(a, b, dims, precision=None):
    return lax.dot_general(
        a, b, (dims, ((), ())), precision=precision, preferred_element_type=F32
    )


def split(a):
    high = a.astype(BF16)
    return high, (a - high.astype(F32)).astype(BF16)


def cube(inner):
    shifted = inner + 1.0
    return (shifted * shifted * shifted).astype(BF16)


def three(a):
    high = a.astype(BF16).astype(F32)
    rest = a - high
    middle = rest.astype(BF16).astype(F32)
    return high, middle, rest - middle


def factor_inverse(rows, n, jobs):
    blocks = n // 8
    lane = lax.broadcasted_iota(jnp.int32, (8, n), 1)
    sub = lax.broadcasted_iota(jnp.int32, (8, n), 0)
    rows = list(rows)
    done = []

    def row_of(a, t):
        return jnp.broadcast_to(a[t : t + 1, :], (8, n))

    for g in range(blocks):
        first = 8 * g
        inside = (lane >= first) & (lane < first + 8)
        pivot = jnp.where(inside, jnp.where(lane == sub + first, 1.0, 0.0), rows[g])
        near = min(g + 2, blocks) - g
        column = [
            [jnp.broadcast_to(rows[g + v][:, first + k : first + k + 1], (8, n)) for k in range(8)]
            for v in range(near)
        ]
        factor = [None] * 8
        diagonal = jnp.zeros((8, n), F32)
        if jobs:
            jobs.pop(0)()
        for t in range(8):
            diagonal = jnp.where(sub == t, column[0][t], diagonal)
            r = row_of(1.0 / column[0][t], t)
            own = jnp.where(sub > t, column[0][t] * r, 0.0)
            if near > 1:
                factor[t] = column[1][t] * r
            for k in range(t + 1, 8):
                e = row_of(column[0][k], t)
                column[0][k] = column[0][k] - own * e
                if near > 1:
                    column[1][k] = column[1][k] - factor[t] * e
            pivot = pivot - own * row_of(pivot, t)
        if g + 2 < blocks:
            a1, a2, a3 = three(pivot * (1.0 / diagonal))
            b1, b2, b3 = three(pivot)
            left = jnp.concatenate([a1, a1, a2, a2, a1, a3], axis=0).astype(BF16)
            right = jnp.concatenate([b1, b2, b1, b2, b3, b1], axis=0).astype(BF16)
            update = mm(left, right, TN)
            for v in range(g + 2, blocks):
                rows[v] = jnp.where(inside, 0.0, rows[v]) - update[8 * v : 8 * v + 8, :]
        if near > 1:
            m = jnp.where(inside, 0.0, rows[g + 1])
            for t in range(8):
                m = m - factor[t] * row_of(pivot, t)
            rows[g + 1] = m
        done.append(jnp.where(lane <= sub + first, pivot, 0.0) * lax.rsqrt(diagonal))
    return jnp.concatenate(done, axis=0)


def inverse_factor(gram, jobs, base=128):
    n = gram.shape[0]
    if n <= base:
        return factor_inverse([gram[8 * i : 8 * i + 8, :] for i in range(n // 8)], n, jobs)
    k = n // 2
    high = lax.Precision.HIGHEST
    w11 = inverse_factor(gram[:k, :k], jobs, base)
    l21 = mm(gram[k:, :k], w11, NT, high)
    w22 = inverse_factor(gram[k:, k:] - mm(l21, l21, NT, high), jobs, base)
    w21 = -mm(w22, mm(l21, w11, NN, high), NN, high)
    top = jnp.concatenate([w11, jnp.zeros((k, n - k), F32)], axis=1)
    return jnp.concatenate([top, jnp.concatenate([w21, w22], axis=1)], axis=0)


def sketch_kernel(scale, x_ref, y_ref, t_ref, mine_ref, given_ref, pairs_ref, x4, total):
    step = pl.program_id(0)

    @pl.when(step == 0)
    def _():
        pairs = jnp.concatenate(split(x_ref[...] * scale), axis=0).T
        x4[...] = jnp.concatenate([pairs, pairs], axis=1)
        pairs_ref[...] = pairs
        total[...] = jnp.zeros_like(total)

    high, low = split(y_ref[...])
    y4 = jnp.concatenate([high, high, low, low], axis=0)
    sub = 256
    for i in range(total.shape[0] // sub):
        there = slice(i * sub, (i + 1) * sub)
        total[there, :] += mm(cube(mm(x4[there, :], y4, NN)), t_ref[...], NN)

    @pl.when(step == pl.num_programs(0) - 1)
    def _():
        half = mine_ref.shape[0]
        core = lax.axis_index("cols") % 2
        mine_ref[...] = total[pl.ds(pl.multiple_of(core * half, half), half), :]
        given_ref[...] = total[pl.ds(pl.multiple_of((1 - core) * half, half), half), :]


def sketch_call(x_t, y_t, test, scale):
    width, rows = x_t.shape
    cols, columns = test.shape
    tile = 2048
    whole = lambda shape: pl.BlockSpec(shape, lambda j: (0, 0))
    return pl.pallas_call(
        lambda *refs: sketch_kernel(scale, *refs),
        grid=(cols // tile,),
        in_specs=[
            whole((width, rows)),
            pl.BlockSpec((width, tile), lambda j: (0, j)),
            pl.BlockSpec((tile, columns), lambda j: (j, 0)),
        ],
        out_specs=[
            whole((rows // 2, columns)),
            whole((rows // 2, columns)),
            whole((rows, 2 * width)),
        ],
        out_shape=[
            jax.ShapeDtypeStruct((rows // 2, columns), F32),
            jax.ShapeDtypeStruct((rows // 2, columns), F32),
            jax.ShapeDtypeStruct((rows, 2 * width), BF16),
        ],
        scratch_shapes=[pltpu.VMEM((rows, 4 * width), BF16), pltpu.VMEM((rows, columns), F32)],
        name="sketch_tile",
    )(x_t, y_t, test)


def pieces_kernel(mine_ref, there_ref, *out_refs):
    quarter = out_refs[0].shape[0]
    iy = lax.axis_index("cols") // 2
    for d, out_ref in enumerate(out_refs):
        rows = pl.ds(pl.multiple_of((iy ^ d) * quarter, quarter), quarter)
        out_ref[...] = mine_ref[rows, :] + there_ref[rows, :]


def pieces_call(mine, there, count):
    shape = jax.ShapeDtypeStruct((mine.shape[0] // count, mine.shape[1]), F32)
    return pl.pallas_call(pieces_kernel, out_shape=[shape] * count, name="chip_sums")(mine, there)


def columns_kernel(y_ref, y4_ref):
    cols = y4_ref.shape[0]
    start = (lax.axis_index("rows") % 2) * cols
    high, low = split(y_ref[:, pl.ds(pl.multiple_of(start, cols), cols)])
    y4_ref[...] = jnp.concatenate([high, high, low, low], axis=0).T


def columns_call(y_t):
    width, cols = y_t.shape
    return pl.pallas_call(
        columns_kernel,
        out_shape=jax.ShapeDtypeStruct((cols // 2, 4 * width), BF16),
        cost_estimate=pl.CostEstimate(
            flops=0, bytes_accessed=4 * y_t.size + 4 * width * cols, transcendentals=0
        ),
        name="column_pieces",
    )(y_t)


def rows_of_kernel(y4, piece, columns):
    pairs = piece[:, columns:]
    k = cube(mm(y4, jnp.concatenate([pairs, pairs], axis=1), NT))
    return mm(k, piece[:, :columns], NN)


def gram_of(pieces, columns, total=None):
    for piece in pieces:
        s = piece[:, :columns]
        part = mm(s, s, TN)
        total = part if total is None else total + part
    return total


def gram_kernel(columns, count, first, *refs):
    refs, g_ref = refs[:-1], refs[-1]
    g_ref[...] = gram_of(refs[:count], columns, None if first else refs[count][...])


def gram_call(pieces, columns, carry=None):
    first = carry is None
    return pl.pallas_call(
        lambda *refs: gram_kernel(columns, len(pieces), first, *refs),
        out_shape=jax.ShapeDtypeStruct((columns, columns), F32),
        cost_estimate=pl.CostEstimate(
            flops=2 * columns * columns * sum(a.shape[0] for a in pieces),
            bytes_accessed=2 * sum(a.size for a in pieces) + 8 * columns * columns,
            transcendentals=0,
        ),
        name="sketch_gram",
    )(*pieces, *(() if first else (carry,)))


def final_kernel(places, early, count, *refs):
    parts, refs = refs[:count], refs[count:]
    (y4_ref, g_ref), refs = refs[:2], refs[2:]
    basis_ref, projected_ref, given_ref, w, s, z = refs
    columns = g_ref.shape[0]
    cols = z.shape[0]
    quarter = s.shape[0] // len(places)
    for place, piece in places:
        rows = pl.ds(pl.multiple_of(place() * quarter, quarter), quarter)
        s[rows, :] = parts[piece][:quarter, :columns]
    gram = gram_of(parts[early:], columns, g_ref[...])

    sub = 256
    work = [(i, n) for i in range(cols // sub) for n in range(count)]
    slots = columns // 8

    def job(part):
        def run():
            for i, n in part:
                there = slice(i * sub, (i + 1) * sub)
                term = rows_of_kernel(y4_ref[there, :], parts[n], columns)
                z[there, :] = term if n == 0 else z[there, :] + term

        return run

    bounds = [len(work) * i // slots for i in range(slots + 1)]
    jobs = [job(work[i:j]) for i, j in zip(bounds, bounds[1:])]
    w[...] = inverse_factor(gram, jobs)

    own_r, own_c = projected_ref.shape[0], basis_ref.shape[0]
    ir, ic = lax.axis_index("rows"), lax.axis_index("cols")

    def rows_of(i, n):
        return split(w[pl.ds(pl.multiple_of(i * n, n), n), :])

    mine, given = rows_of(ir, own_r), rows_of(ir ^ 1, own_r)
    tall = jnp.concatenate([mine[0], given[0], mine[1], given[1]], axis=0)
    start = (ir % 2) * cols
    tile = 512
    for j in range(cols // tile):
        high, low = split(z[tile * j : tile * (j + 1), :])
        both = mm(tall, high, NT)
        both = both[: 2 * own_r] + both[2 * own_r :] + mm(tall[: 2 * own_r], low, NT)
        there = pl.ds(pl.multiple_of(start + tile * j, tile), tile)
        projected_ref[:, there] = both[:own_r]
        given_ref[:, tile * j : tile * (j + 1)] = both[own_r:].astype(BF16)
    both = mm(jnp.concatenate(rows_of(ic, own_c), axis=0), s[...], NT)
    basis_ref[...] = both[:own_c] + both[own_c:]


def final_call(parts, early, y4, gram, places, quarter, own_r, own_c):
    columns = gram.shape[0]
    whole = lambda shape: pl.BlockSpec(shape, lambda i: (0, 0))
    height = quarter * len(places)
    cols = y4.shape[0]
    return pl.pallas_call(
        lambda *refs: final_kernel(places, early, len(parts), *refs),
        grid=(1,),
        in_specs=[whole(a.shape) for a in parts] + [whole(y4.shape), whole(gram.shape)],
        out_specs=[whole((own_c, height)), whole((own_r, 2 * cols)), whole((own_r, cols))],
        out_shape=[
            jax.ShapeDtypeStruct((own_c, height), F32),
            jax.ShapeDtypeStruct((own_r, 2 * cols), F32),
            jax.ShapeDtypeStruct((own_r, cols), BF16),
        ],
        scratch_shapes=[
            pltpu.VMEM((columns, columns), F32),
            pltpu.VMEM((height, columns), BF16),
            pltpu.VMEM((cols, columns), F32),
        ],
        name="factor_and_project",
    )(*parts, y4, gram)


def swap(a, axis, bits):
    return lax.ppermute(a, axis, [(i, i ^ bits) for i in range(lax.axis_size(axis))])


def local(row_features, col_features, test_block):
    cols = lax.axis_size("cols")
    rows = lax.axis_size("rows")
    chips_y, chips_z = cols // 2, rows // 2
    ir, ic = lax.axis_index("rows"), lax.axis_index("cols")
    core, iy = ic % 2, ic // 2
    height, width = row_features.shape
    scale = 1.0 / math.sqrt(width)
    columns = test_block.shape[1]
    half = height // 2
    quarter = half // chips_y

    x_t, y_t = row_features.T, col_features.T
    mine, given, pairs = sketch_call(x_t, y_t, test_block, scale)
    y4 = columns_call(y_t)
    s_own, *given = pieces_call(mine, swap(given, "cols", 1), chips_y)
    for d in range(1, chips_y):
        s_own = s_own + swap(given[d - 1], "cols", 2 * d)
    pairs = lax.dynamic_slice_in_dim(pairs, core * half + iy * quarter, quarter, 0)
    piece = jnp.concatenate([s_own.astype(BF16), pairs], axis=1)

    along_z = {0: piece}
    for d in range(1, chips_z):
        along_z[d] = swap(piece, "rows", 2 * d)
    own = jnp.concatenate([along_z[d] for d in range(chips_z)], 0)
    near_x = swap(own, "rows", 1)
    near_y = [swap(own, "cols", 2 * d) for d in range(1, chips_y)]
    own_core = swap(own, "cols", 1)
    gram = gram_call([own, own_core], columns)
    cut = own.shape[0] // 2
    far = []
    for d in range(1, chips_y):
        far.append(swap(near_y[d - 1][:cut], "rows", 1))
        far.append(swap(near_x[cut:], "cols", 2 * d))
    near = [near_x] + near_y
    near_core = [swap(a, "cols", 1) for a in near]
    gram = gram_call(near, columns, gram)
    parts = [own, own_core] + near
    early = len(parts)
    parts += near_core + far + [swap(a, "cols", 1) for a in far]

    places = []
    for k, group in enumerate(([0] + list(range(3, early)), [1] + list(range(early + 1, 2 * early - 2)))):
        for d, n in enumerate(group):

            def place(k=k, d=d):
                c = lax.axis_index("cols")
                return ((c % 2) ^ k) * chips_y + ((c // 2) ^ d)

            places.append((place, n))
    basis_t, projected, given = final_call(
        parts, early, y4, gram, places, quarter, columns // rows, columns // cols
    )
    there = swap(given, "rows", 1).astype(F32)
    projected = lax.dynamic_update_slice_in_dim(
        projected, there, (1 - ir % 2) * there.shape[1], 1
    )
    return (basis_t.T, projected)


def solution(mesh):
    in_specs = (P("rows", None), P("cols", None), P("cols", None))
    out_specs = (P("rows", "cols"), P("rows", "cols"))
    return jax.shard_map(local, mesh=mesh, in_specs=in_specs, out_specs=out_specs, check_vma=False)
```

```python
import math

import jax
import jax.numpy as jnp
from jax import lax
from jax.experimental import pallas as pl
from jax.experimental.pallas import tpu as pltpu
from jax.sharding import PartitionSpec as P


F32 = jnp.float32
BF16 = jnp.bfloat16
NN = ((1,), (0,))
NT = ((1,), (1,))
TN = ((0,), (0,))


def mm(a, b, dims, precision=None):
    return lax.dot_general(
        a, b, (dims, ((), ())), precision=precision, preferred_element_type=F32
    )


def split(a):
    high = a.astype(BF16)
    return high, (a - high.astype(F32)).astype(BF16)


def cube(inner):
    shifted = inner + 1.0
    return (shifted * shifted * shifted).astype(BF16)


def three(a):
    high = a.astype(BF16).astype(F32)
    rest = a - high
    middle = rest.astype(BF16).astype(F32)
    return high, middle, rest - middle


def factor_inverse(rows, n, jobs):
    blocks = n // 8
    lane = lax.broadcasted_iota(jnp.int32, (8, n), 1)
    sub = lax.broadcasted_iota(jnp.int32, (8, n), 0)
    rows = list(rows)
    done = []

    def row_of(a, t):
        return jnp.broadcast_to(a[t : t + 1, :], (8, n))

    for g in range(blocks):
        first = 8 * g
        inside = (lane >= first) & (lane < first + 8)
        pivot = jnp.where(inside, jnp.where(lane == sub + first, 1.0, 0.0), rows[g])
        near = min(g + 2, blocks) - g
        column = [
            [jnp.broadcast_to(rows[g + v][:, first + k : first + k + 1], (8, n)) for k in range(8)]
            for v in range(near)
        ]
        factor = [None] * 8
        diagonal = jnp.zeros((8, n), F32)
        if jobs:
            jobs.pop(0)()
        for t in range(8):
            diagonal = jnp.where(sub == t, column[0][t], diagonal)
            r = row_of(1.0 / column[0][t], t)
            own = jnp.where(sub > t, column[0][t] * r, 0.0)
            if near > 1:
                factor[t] = column[1][t] * r
            for k in range(t + 1, 8):
                e = row_of(column[0][k], t)
                column[0][k] = column[0][k] - own * e
                if near > 1:
                    column[1][k] = column[1][k] - factor[t] * e
            pivot = pivot - own * row_of(pivot, t)
        if g + 2 < blocks:
            a1, a2, a3 = three(pivot * (1.0 / diagonal))
            b1, b2, b3 = three(pivot)
            left = jnp.concatenate([a1, a1, a2, a2, a1, a3], axis=0).astype(BF16)
            right = jnp.concatenate([b1, b2, b1, b2, b3, b1], axis=0).astype(BF16)
            update = mm(left, right, TN)
            for v in range(g + 2, blocks):
                rows[v] = jnp.where(inside, 0.0, rows[v]) - update[8 * v : 8 * v + 8, :]
        if near > 1:
            m = jnp.where(inside, 0.0, rows[g + 1])
            for t in range(8):
                m = m - factor[t] * row_of(pivot, t)
            rows[g + 1] = m
        done.append(jnp.where(lane <= sub + first, pivot, 0.0) * lax.rsqrt(diagonal))
    return jnp.concatenate(done, axis=0)


def inverse_factor(gram, jobs, base=128):
    n = gram.shape[0]
    if n <= base:
        return factor_inverse([gram[8 * i : 8 * i + 8, :] for i in range(n // 8)], n, jobs)
    k = n // 2
    high = lax.Precision.HIGHEST
    w11 = inverse_factor(gram[:k, :k], jobs, base)
    l21 = mm(gram[k:, :k], w11, NT, high)
    w22 = inverse_factor(gram[k:, k:] - mm(l21, l21, NT, high), jobs, base)
    w21 = -mm(w22, mm(l21, w11, NN, high), NN, high)
    top = jnp.concatenate([w11, jnp.zeros((k, n - k), F32)], axis=1)
    return jnp.concatenate([top, jnp.concatenate([w21, w22], axis=1)], axis=0)


def sketch_kernel(scale, quarter, x_ref, y_ref, t_ref, mine_ref, given_ref, own_ref, x4, total):
    step = pl.program_id(0)

    @pl.when(step == 0)
    def _():
        pairs = jnp.concatenate(split(x_ref[...] * scale), axis=0).T
        x4[...] = jnp.concatenate([pairs, pairs], axis=1)
        depth, columns = own_ref.shape
        width = x_ref.shape[0]
        c = lax.axis_index("cols")
        start = (c % 2) * (total.shape[0] // 2) + (c // 2) * quarter
        packed = []
        for b in range(columns // width):
            if b * depth < quarter:
                rows = pl.ds(pl.multiple_of(start + b * depth, depth), depth)
                packed.append(x4[rows, :][:, :width])
            else:
                packed.append(jnp.zeros((depth, width), BF16))
        own_ref[...] = jnp.concatenate(packed, axis=1)
        total[...] = jnp.zeros_like(total)

    high, low = split(y_ref[...])
    y4 = jnp.concatenate([high, high, low, low], axis=0)
    sub = 256
    for i in range(total.shape[0] // sub):
        there = slice(i * sub, (i + 1) * sub)
        total[there, :] += mm(cube(mm(x4[there, :], y4, NN)), t_ref[...], NN)

    @pl.when(step == pl.num_programs(0) - 1)
    def _():
        half = mine_ref.shape[0]
        core = lax.axis_index("cols") % 2
        mine_ref[...] = total[pl.ds(pl.multiple_of(core * half, half), half), :]
        given_ref[...] = total[pl.ds(pl.multiple_of((1 - core) * half, half), half), :]


def sketch_call(x_t, y_t, test, scale, quarter, depth):
    width, rows = x_t.shape
    cols, columns = test.shape
    tile = 2048
    whole = lambda shape: pl.BlockSpec(shape, lambda j: (0, 0))
    return pl.pallas_call(
        lambda *refs: sketch_kernel(scale, quarter, *refs),
        grid=(cols // tile,),
        in_specs=[
            whole((width, rows)),
            pl.BlockSpec((width, tile), lambda j: (0, j)),
            pl.BlockSpec((tile, columns), lambda j: (j, 0)),
        ],
        out_specs=[
            whole((rows // 2, columns)),
            whole((rows // 2, columns)),
            whole((depth, columns)),
        ],
        out_shape=[
            jax.ShapeDtypeStruct((rows // 2, columns), F32),
            jax.ShapeDtypeStruct((rows // 2, columns), F32),
            jax.ShapeDtypeStruct((depth, columns), BF16),
        ],
        scratch_shapes=[pltpu.VMEM((rows, 4 * width), BF16), pltpu.VMEM((rows, columns), F32)],
        name="sketch_tile",
    )(x_t, y_t, test)


def columns_kernel(y_ref, y2_ref):
    cols = y2_ref.shape[0]
    start = (lax.axis_index("rows") % 2) * cols
    high, low = split(y_ref[:, pl.ds(pl.multiple_of(start, cols), cols)])
    y2_ref[...] = jnp.concatenate([high, low], axis=0).T


def columns_call(y_t):
    width, cols = y_t.shape
    return pl.pallas_call(
        columns_kernel,
        out_shape=jax.ShapeDtypeStruct((cols // 2, 2 * width), BF16),
        cost_estimate=pl.CostEstimate(
            flops=0, bytes_accessed=4 * y_t.size + 4 * width * cols, transcendentals=0
        ),
        name="column_pieces",
    )(y_t)


def sketch_rows(parts, quarter, depth):
    return jnp.concatenate(
        [a[j : j + quarter, :] for a in parts for j in range(0, a.shape[0], quarter + depth)], axis=0
    )


def gram_of(sketches, total=None):
    for s in sketches:
        part = mm(s, s, TN)
        total = part if total is None else total + part
    return total


def gram_kernel(quarter, depth, count, first, *refs):
    refs, g_ref = refs[:-1], refs[-1]
    sketches = [sketch_rows([a], quarter, depth) for a in refs[:count]]
    g_ref[...] = gram_of(sketches, None if first else refs[count][...])


def gram_call(pieces, quarter, depth, carry=None):
    columns = pieces[0].shape[1]
    first = carry is None
    return pl.pallas_call(
        lambda *refs: gram_kernel(quarter, depth, len(pieces), first, *refs),
        out_shape=jax.ShapeDtypeStruct((columns, columns), F32),
        cost_estimate=pl.CostEstimate(
            flops=2 * columns * columns * sum(a.shape[0] for a in pieces),
            bytes_accessed=2 * sum(a.size for a in pieces) + 8 * columns * columns,
            transcendentals=0,
        ),
        name="sketch_gram",
    )(*pieces, *(() if first else (carry,)))


def final_kernel(places, depth, early, groups, *refs):
    count = sum(groups)
    parts, refs = refs[:count], refs[count:]
    (y2_ref, g_ref), refs = refs[:2], refs[2:]
    basis_ref, projected_ref, given_ref, w, s, z, x2 = refs
    columns = g_ref.shape[0]
    cols = z.shape[0]
    width = y2_ref.shape[1] // 2
    quarter = s.shape[0] // len(places)
    for place, piece in places:
        rows = pl.ds(pl.multiple_of(place() * quarter, quarter), quarter)
        s[rows, :] = parts[piece][:quarter, :]
    sources, first = [], 0
    for n in groups:
        sources.append(parts[first : first + n])
        first += n

    def sketch(n):
        return sketch_rows(sources[n], quarter, depth)

    def features(n):
        rows = []
        for part in sources[n]:
            for j in range(quarter, part.shape[0], quarter + depth):
                packed = part[j : j + depth, :]
                for b in range(quarter // depth):
                    a = packed[:, b * width : (b + 1) * width]
                    rows.append(jnp.concatenate([a, a], axis=1))
        return jnp.concatenate(rows, axis=0)

    gram = gram_of([sketch(n) for n in range(early, len(groups))], g_ref[...])

    sub = 256
    work = [(i, n) for i in range(cols // sub) for n in range(len(groups))]
    slots = columns // 8

    def job(part):
        def run():
            for i, n in part:
                there = slice(i * sub, (i + 1) * sub)
                if i == 0:
                    x2[n] = features(n)
                term = mm(cube(mm(y2_ref[there, :], x2[n], NT)), sketch(n), NN)
                z[there, :] = term if n == 0 else z[there, :] + term

        return run

    bounds = [len(work) * i // slots for i in range(slots + 1)]
    jobs = [job(work[i:j]) for i, j in zip(bounds, bounds[1:])]
    w[...] = inverse_factor(gram, jobs)

    own_r, own_c = projected_ref.shape[0], basis_ref.shape[0]
    ir, ic = lax.axis_index("rows"), lax.axis_index("cols")

    def rows_of(i, n):
        return split(w[pl.ds(pl.multiple_of(i * n, n), n), :])

    mine, given = rows_of(ir, own_r), rows_of(ir ^ 1, own_r)
    tall = jnp.concatenate([mine[0], given[0], mine[1], given[1]], axis=0)
    start = (ir % 2) * cols
    tile = 512
    for j in range(cols // tile):
        high, low = split(z[tile * j : tile * (j + 1), :])
        both = mm(tall, high, NT)
        both = both[: 2 * own_r] + both[2 * own_r :] + mm(tall[: 2 * own_r], low, NT)
        there = pl.ds(pl.multiple_of(start + tile * j, tile), tile)
        projected_ref[:, there] = both[:own_r]
        given_ref[:, tile * j : tile * (j + 1)] = both[own_r:].astype(BF16)
    both = mm(jnp.concatenate(rows_of(ic, own_c), axis=0), s[...], NT)
    basis_ref[...] = both[:own_c] + both[own_c:]


def final_call(groups, early, y2, gram, places, quarter, depth, own_r, own_c):
    columns = gram.shape[0]
    parts = [a for group in groups for a in group]
    counts = [len(group) for group in groups]
    whole = lambda shape: pl.BlockSpec(shape, lambda i: (0, 0))
    height = quarter * len(places)
    cols = y2.shape[0]
    return pl.pallas_call(
        lambda *refs: final_kernel(places, depth, early, counts, *refs),
        grid=(1,),
        in_specs=[whole(a.shape) for a in parts] + [whole(y2.shape), whole(gram.shape)],
        out_specs=[whole((own_c, height)), whole((own_r, 2 * cols)), whole((own_r, cols))],
        out_shape=[
            jax.ShapeDtypeStruct((own_c, height), F32),
            jax.ShapeDtypeStruct((own_r, 2 * cols), F32),
            jax.ShapeDtypeStruct((own_r, cols), BF16),
        ],
        scratch_shapes=[
            pltpu.VMEM((columns, columns), F32),
            pltpu.VMEM((height, columns), BF16),
            pltpu.VMEM((cols, columns), F32),
            pltpu.VMEM((len(groups), sum(a.shape[0] for a in groups[0]) // (quarter + depth) * quarter, y2.shape[1]), BF16),
        ],
        name="factor_and_project",
    )(*parts, y2, gram)


def swap(a, axis, bits):
    return lax.ppermute(a, axis, [(i, i ^ bits) for i in range(lax.axis_size(axis))])


def local(row_features, col_features, test_block):
    cols = lax.axis_size("cols")
    rows = lax.axis_size("rows")
    chips_y, chips_z = cols // 2, rows // 2
    ir, ic = lax.axis_index("rows"), lax.axis_index("cols")
    iy = ic // 2
    height, width = row_features.shape
    scale = 1.0 / math.sqrt(width)
    columns = test_block.shape[1]
    half = height // 2
    quarter = half // chips_y

    x_t, y_t = row_features.T, col_features.T
    depth = max(16, quarter * width // columns)
    mine, given, x_own = sketch_call(x_t, y_t, test_block, scale, quarter, depth)
    y2 = columns_call(y_t)
    mine = mine + swap(given, "cols", 1)
    s_own = lax.dynamic_slice_in_dim(mine, iy * quarter, quarter, 0)
    for d in range(1, chips_y):
        given = lax.dynamic_slice_in_dim(mine, (iy ^ d) * quarter, quarter, 0)
        s_own = s_own + swap(given, "cols", 2 * d)
    piece = jnp.concatenate([s_own.astype(BF16), x_own], axis=0)

    along_z = {0: piece}
    for d in range(1, chips_z):
        along_z[d] = swap(piece, "rows", 2 * d)
    own = jnp.concatenate([along_z[d] for d in range(chips_z)], 0)
    near_x = swap(own, "rows", 1)
    near_y = [swap(own, "cols", 2 * d) for d in range(1, chips_y)]
    own_core = swap(own, "cols", 1)
    gram = gram_call([own, own_core], quarter, depth)
    cut = own.shape[0] // 2
    far = []
    for d in range(1, chips_y):
        low = swap(near_y[d - 1][:cut], "rows", 1)
        far.append([low, swap(near_x[cut:], "cols", 2 * d)])
    near = [near_x] + near_y
    near_core = [swap(a, "cols", 1) for a in near]
    gram = gram_call(near + near_core, quarter, depth, gram)
    singles = [own, own_core] + near + near_core
    early = len(singles)
    groups = [[a] for a in singles] + far + [[swap(a, "cols", 1) for a in pair] for pair in far]

    places = []
    with_y = len(near)
    for k, group in enumerate(
        (
            [0] + list(range(3, 2 + with_y)),
            [1] + list(range(3 + with_y, 2 + 2 * with_y)),
        )
    ):
        for d, n in enumerate(group):

            def place(k=k, d=d):
                c = lax.axis_index("cols")
                return ((c % 2) ^ k) * chips_y + ((c // 2) ^ d)

            places.append((place, n))
    basis_t, projected, given = final_call(
        groups, early, y2, gram, places, quarter, depth, columns // rows, columns // cols
    )
    there = swap(given, "rows", 1).astype(F32)
    projected = lax.dynamic_update_slice_in_dim(
        projected, there, (1 - ir % 2) * there.shape[1], 1
    )
    return (basis_t.T, projected)


def solution(mesh):
    in_specs = (P("rows", None), P("cols", None), P("cols", None))
    out_specs = (P("rows", "cols"), P("rows", "cols"))
    return jax.shard_map(local, mesh=mesh, in_specs=in_specs, out_specs=out_specs, check_vma=False)
```

```python
import math

import jax
import jax.numpy as jnp
from jax import lax
from jax.experimental import pallas as pl
from jax.experimental.pallas import tpu as pltpu
from jax.sharding import PartitionSpec as P


F32 = jnp.float32
BF16 = jnp.bfloat16
NN = ((1,), (0,))
NT = ((1,), (1,))
TN = ((0,), (0,))


def mm(a, b, dims, precision=None):
    return lax.dot_general(
        a, b, (dims, ((), ())), precision=precision, preferred_element_type=F32
    )


def split(a):
    high = a.astype(BF16)
    return high, (a - high.astype(F32)).astype(BF16)


def cube(inner):
    shifted = inner + 1.0
    return (shifted * shifted * shifted).astype(BF16)


def three(a):
    high = a.astype(BF16).astype(F32)
    rest = a - high
    middle = rest.astype(BF16).astype(F32)
    return high, middle, rest - middle


def factor_inverse(rows, n, jobs):
    blocks = n // 8
    lane = lax.broadcasted_iota(jnp.int32, (8, n), 1)
    sub = lax.broadcasted_iota(jnp.int32, (8, n), 0)
    rows = list(rows)
    done = []

    def row_of(a, t):
        return jnp.broadcast_to(a[t : t + 1, :], (8, n))

    for g in range(blocks):
        first = 8 * g
        inside = (lane >= first) & (lane < first + 8)
        pivot = jnp.where(inside, jnp.where(lane == sub + first, 1.0, 0.0), rows[g])
        near = min(g + 2, blocks) - g
        column = [
            [jnp.broadcast_to(rows[g + v][:, first + k : first + k + 1], (8, n)) for k in range(8)]
            for v in range(near)
        ]
        factor = [None] * 8
        diagonal = jnp.zeros((8, n), F32)
        if jobs:
            jobs.pop(0)()
        for t in range(0, 8, 2):
            c0, c1 = column[0][t], column[0][t + 1]
            a, b, d = row_of(c0, t), row_of(c1, t), row_of(c1, t + 1)
            det = a * d - b * b
            ra, rdet = 1.0 / a, 1.0 / det
            ratio = b * ra
            diagonal = jnp.where(sub == t, a, jnp.where(sub == t + 1, det * ra, diagonal))
            own0 = jnp.where(sub > t, c0 * ra, 0.0)
            own1 = jnp.where(sub > t + 1, (c1 * a - c0 * b) * rdet, 0.0)
            if near > 1:
                n0, n1 = column[1][t], column[1][t + 1]
                factor[t], factor[t + 1] = n0 * ra, (n1 * a - n0 * b) * rdet
            for k in range(t + 2, 8):
                e0 = row_of(column[0][k], t)
                e1 = row_of(column[0][k], t + 1) - ratio * e0
                column[0][k] = column[0][k] - own0 * e0 - own1 * e1
                if near > 1:
                    column[1][k] = column[1][k] - factor[t] * e0 - factor[t + 1] * e1
            p0 = row_of(pivot, t)
            p1 = row_of(pivot, t + 1) - ratio * p0
            pivot = pivot - own0 * p0 - own1 * p1
        if g + 2 < blocks:
            a1, a2, a3 = three(pivot * (1.0 / diagonal))
            b1, b2, b3 = three(pivot)
            left = jnp.concatenate([a1, a1, a2, a2, a1, a3], axis=0).astype(BF16)
            right = jnp.concatenate([b1, b2, b1, b2, b3, b1], axis=0).astype(BF16)
            update = mm(left, right, TN)
            for v in range(g + 2, blocks):
                rows[v] = jnp.where(inside, 0.0, rows[v]) - update[8 * v : 8 * v + 8, :]
        if near > 1:
            m = jnp.where(inside, 0.0, rows[g + 1])
            for t in range(8):
                m = m - factor[t] * row_of(pivot, t)
            rows[g + 1] = m
        done.append(jnp.where(lane <= sub + first, pivot, 0.0) * lax.rsqrt(diagonal))
    return jnp.concatenate(done, axis=0)


def inverse_factor(gram, jobs, base=128):
    n = gram.shape[0]
    if n <= base:
        return factor_inverse([gram[8 * i : 8 * i + 8, :] for i in range(n // 8)], n, jobs)
    k = n // 2
    high = lax.Precision.HIGHEST
    w11 = inverse_factor(gram[:k, :k], jobs, base)
    l21 = mm(gram[k:, :k], w11, NT, high)
    w22 = inverse_factor(gram[k:, k:] - mm(l21, l21, NT, high), jobs, base)
    w21 = -mm(w22, mm(l21, w11, NN, high), NN, high)
    top = jnp.concatenate([w11, jnp.zeros((k, n - k), F32)], axis=1)
    return jnp.concatenate([top, jnp.concatenate([w21, w22], axis=1)], axis=0)


def sketch_kernel(scale, quarter, x_ref, y_ref, t_ref, own_ref, *refs):
    piece_refs, (x4, total) = refs[:-2], refs[-2:]
    step = pl.program_id(0)
    c = lax.axis_index("cols")

    def first_row(bits):
        i = c ^ bits
        return pl.multiple_of((i % 2) * (total.shape[0] // 2) + (i // 2) * quarter, quarter)


    @pl.when(step == 0)
    def _():
        pairs = jnp.concatenate(split(x_ref[...] * scale), axis=0).T
        x4[...] = jnp.concatenate([pairs, pairs], axis=1)
        depth, columns = own_ref.shape
        width = x_ref.shape[0]
        packed = []
        for b in range(columns // width):
            if b * depth < quarter:
                rows = pl.ds(pl.multiple_of(first_row(0) + b * depth, depth), depth)
                packed.append(x4[rows, :][:, :width])
            else:
                packed.append(jnp.zeros((depth, width), BF16))
        own_ref[...] = jnp.concatenate(packed, axis=1)
        total[...] = jnp.zeros_like(total)

    high, low = split(y_ref[...])
    y4 = jnp.concatenate([high, high, low, low], axis=0)
    sub = 256
    for i in range(total.shape[0] // sub):
        there = slice(i * sub, (i + 1) * sub)
        total[there, :] += mm(cube(mm(x4[there, :], y4, NN)), t_ref[...], NN)

    @pl.when(step == pl.num_programs(0) - 1)
    def _():
        for bits, piece_ref in enumerate(piece_refs):
            piece_ref[...] = total[pl.ds(first_row(bits), quarter), :].astype(piece_ref.dtype)


def sketch_call(x_t, y_t, test, scale, quarter, depth):
    width, rows = x_t.shape
    cols, columns = test.shape
    tile = 2048
    whole = lambda shape: pl.BlockSpec(shape, lambda j: (0, 0))
    count = rows // quarter
    types = [F32 if bits < 2 else BF16 for bits in range(count)]
    return pl.pallas_call(
        lambda *refs: sketch_kernel(scale, quarter, *refs),
        grid=(cols // tile,),
        in_specs=[
            whole((width, rows)),
            pl.BlockSpec((width, tile), lambda j: (0, j)),
            pl.BlockSpec((tile, columns), lambda j: (j, 0)),
        ],
        out_specs=[
            whole((depth, columns)),
        ]
        + [whole((quarter, columns))] * count,
        out_shape=[jax.ShapeDtypeStruct((depth, columns), BF16)]
        + [jax.ShapeDtypeStruct((quarter, columns), t) for t in types],
        scratch_shapes=[pltpu.VMEM((rows, 4 * width), BF16), pltpu.VMEM((rows, columns), F32)],
        name="sketch_tile",
    )(x_t, y_t, test)


def columns_kernel(y_ref, y2_ref):
    cols = y2_ref.shape[0]
    start = (lax.axis_index("rows") % 2) * cols
    high, low = split(y_ref[:, pl.ds(pl.multiple_of(start, cols), cols)])
    y2_ref[...] = jnp.concatenate([high, low], axis=0).T


def columns_call(y_t):
    width, cols = y_t.shape
    return pl.pallas_call(
        columns_kernel,
        out_shape=jax.ShapeDtypeStruct((cols // 2, 2 * width), BF16),
        cost_estimate=pl.CostEstimate(
            flops=0, bytes_accessed=4 * y_t.size + 4 * width * cols, transcendentals=0
        ),
        name="column_pieces",
    )(y_t)


def sketch_rows(parts, quarter, depth):
    return jnp.concatenate(
        [a[j : j + quarter, :] for a in parts for j in range(0, a.shape[0], quarter + depth)], axis=0
    )


def gram_of(sketches, total=None):
    for s in sketches:
        part = mm(s, s, TN)
        total = part if total is None else total + part
    return total


def gram_kernel(quarter, depth, count, first, *refs):
    refs, g_ref = refs[:-1], refs[-1]
    sketches = [sketch_rows([a], quarter, depth) for a in refs[:count]]
    g_ref[...] = gram_of(sketches, None if first else refs[count][...])


def gram_call(pieces, quarter, depth, carry=None):
    columns = pieces[0].shape[1]
    first = carry is None
    return pl.pallas_call(
        lambda *refs: gram_kernel(quarter, depth, len(pieces), first, *refs),
        out_shape=jax.ShapeDtypeStruct((columns, columns), F32),
        cost_estimate=pl.CostEstimate(
            flops=2 * columns * columns * sum(a.shape[0] for a in pieces),
            bytes_accessed=2 * sum(a.size for a in pieces) + 8 * columns * columns,
            transcendentals=0,
        ),
        name="sketch_gram",
    )(*pieces, *(() if first else (carry,)))


def final_kernel(places, depth, early, late, groups, *refs):
    count = sum(groups)
    parts, refs = refs[:count], refs[count:]
    (y2_ref, g_ref), refs = refs[:2], refs[2:]
    basis_ref, projected_ref, given_ref, w, s, z, x2, *landed, arrived = refs
    copies = []
    for i, a in enumerate(landed):
        copies.append(pltpu.make_async_copy(parts[count - len(landed) + i], a, arrived.at[i]))
        copies[-1].start()
    parts = parts[: count - len(landed)] + tuple(landed)
    columns = g_ref.shape[0]
    cols = z.shape[0]
    width = y2_ref.shape[1] // 2
    quarter = s.shape[0] // len(places)
    for place, piece in places:
        rows = pl.ds(pl.multiple_of(place() * quarter, quarter), quarter)
        s[rows, :] = parts[piece][:quarter, :]
    sources, first = [], 0
    for n in groups:
        sources.append(parts[first : first + n])
        first += n

    def sketch(n):
        return sketch_rows(sources[n], quarter, depth)

    def features(n):
        rows = []
        for part in sources[n]:
            for j in range(quarter, part.shape[0], quarter + depth):
                packed = part[j : j + depth, :]
                for b in range(quarter // depth):
                    a = packed[:, b * width : (b + 1) * width]
                    rows.append(jnp.concatenate([a, a], axis=1))
        return jnp.concatenate(rows, axis=0)

    gram = gram_of([sketch(n) for n in range(early, late)], g_ref[...])
    for copy in copies:
        copy.wait()
    gram = gram_of([sketch(n) for n in range(late, len(groups))], gram)

    sub = 256
    work = [(i, n) for i in range(cols // sub) for n in range(len(groups))]
    slots = columns // 8

    def job(part):
        def run():
            for i, n in part:
                there = slice(i * sub, (i + 1) * sub)
                if i == 0:
                    x2[n] = features(n)
                term = mm(cube(mm(y2_ref[there, :], x2[n], NT)), sketch(n), NN)
                z[there, :] = term if n == 0 else z[there, :] + term

        return run

    bounds = [len(work) * i // slots for i in range(slots + 1)]
    jobs = [job(work[i:j]) for i, j in zip(bounds, bounds[1:])]
    w[...] = inverse_factor(gram, jobs)

    own_r, own_c = projected_ref.shape[0], basis_ref.shape[0]
    ir, ic = lax.axis_index("rows"), lax.axis_index("cols")

    def rows_of(i, n):
        return split(w[pl.ds(pl.multiple_of(i * n, n), n), :])

    mine, given = rows_of(ir, own_r), rows_of(ir ^ 1, own_r)
    tall = jnp.concatenate([mine[0], given[0], mine[1], given[1]], axis=0)
    start = (ir % 2) * cols
    tile = 512
    for j in range(cols // tile):
        high, low = split(z[tile * j : tile * (j + 1), :])
        both = mm(tall, high, NT)
        both = both[: 2 * own_r] + both[2 * own_r :] + mm(tall[: 2 * own_r], low, NT)
        there = pl.ds(pl.multiple_of(start + tile * j, tile), tile)
        projected_ref[:, there] = both[:own_r]
        given_ref[:, tile * j : tile * (j + 1)] = both[own_r:].astype(BF16)
    both = mm(jnp.concatenate(rows_of(ic, own_c), axis=0), s[...], NT)
    basis_ref[...] = both[:own_c] + both[own_c:]


def final_call(groups, early, late, y2, gram, places, quarter, depth, own_r, own_c):
    columns = gram.shape[0]
    parts = [a for group in groups for a in group]
    counts = [len(group) for group in groups]
    landing = parts[sum(counts[:late]) :]
    whole = lambda shape: pl.BlockSpec(shape, lambda i: (0, 0))
    height = quarter * len(places)
    cols = y2.shape[0]
    return pl.pallas_call(
        lambda *refs: final_kernel(places, depth, early, late, counts, *refs),
        grid=(1,),
        in_specs=[whole(a.shape) for a in parts[: len(parts) - len(landing)]]
        + [pl.BlockSpec(memory_space=pltpu.HBM) for _ in landing]
        + [whole(y2.shape), whole(gram.shape)],
        out_specs=[whole((own_c, height)), whole((own_r, 2 * cols)), whole((own_r, cols))],
        out_shape=[
            jax.ShapeDtypeStruct((own_c, height), F32),
            jax.ShapeDtypeStruct((own_r, 2 * cols), F32),
            jax.ShapeDtypeStruct((own_r, cols), BF16),
        ],
        scratch_shapes=[
            pltpu.VMEM((columns, columns), F32),
            pltpu.VMEM((height, columns), BF16),
            pltpu.VMEM((cols, columns), F32),
            pltpu.VMEM((len(groups), sum(a.shape[0] for a in groups[0]) // (quarter + depth) * quarter, y2.shape[1]), BF16),
        ]
        + [pltpu.VMEM(a.shape, BF16) for a in landing]
        + [pltpu.SemaphoreType.DMA((len(landing),))],
        name="factor_and_project",
    )(*parts, y2, gram)


def swap(a, axis, bits):
    return lax.ppermute(a, axis, [(i, i ^ bits) for i in range(lax.axis_size(axis))])


def local(row_features, col_features, test_block):
    cols = lax.axis_size("cols")
    rows = lax.axis_size("rows")
    chips_y, chips_z = cols // 2, rows // 2
    ir = lax.axis_index("rows")
    height, width = row_features.shape
    scale = 1.0 / math.sqrt(width)
    columns = test_block.shape[1]
    half = height // 2
    quarter = half // chips_y

    x_t, y_t = row_features.T, col_features.T
    depth = max(16, quarter * width // columns)
    x_own, s_own, *given = sketch_call(x_t, y_t, test_block, scale, quarter, depth)
    y2 = columns_call(y_t)
    for bits, a in list(enumerate(given, 1))[::-1]:
        s_own = s_own + swap(a, "cols", bits).astype(F32)
    piece = jnp.concatenate([s_own.astype(BF16), x_own], axis=0)

    along_z = {0: piece}
    for d in range(1, chips_z):
        along_z[d] = swap(piece, "rows", 2 * d)
    own = jnp.concatenate([along_z[d] for d in range(chips_z)], 0)
    near_x = swap(own, "rows", 1)
    near_y = [swap(own, "cols", 2 * d) for d in range(1, chips_y)]
    own_core = swap(own, "cols", 1)
    gram = gram_call([own, own_core], quarter, depth)
    cut = own.shape[0] // 2
    far = []
    for d in range(1, chips_y):
        low = swap(near_y[d - 1][:cut], "rows", 1)
        far.append([low, swap(near_x[cut:], "cols", 2 * d)])
    near = [near_x] + near_y
    near_core = [swap(a, "cols", 1) for a in near]
    gram = gram_call(near + near_core, quarter, depth, gram)
    singles = [own, own_core] + near + near_core
    early = len(singles)
    groups = [[a] for a in singles] + far + [[swap(a, "cols", 1) for a in pair] for pair in far]

    places = []
    with_y = len(near)
    for k, group in enumerate(
        (
            [0] + list(range(3, 2 + with_y)),
            [1] + list(range(3 + with_y, 2 + 2 * with_y)),
        )
    ):
        for d, n in enumerate(group):

            def place(k=k, d=d):
                c = lax.axis_index("cols")
                return ((c % 2) ^ k) * chips_y + ((c // 2) ^ d)

            places.append((place, n))
    basis_t, projected, given = final_call(
        groups, early, early + len(far), y2, gram, places, quarter, depth, columns // rows, columns // cols
    )
    there = swap(given, "rows", 1).astype(F32)
    projected = lax.dynamic_update_slice_in_dim(
        projected, there, (1 - ir % 2) * there.shape[1], 1
    )
    return (basis_t.T, projected)


def solution(mesh):
    in_specs = (P("rows", None), P("cols", None), P("cols", None))
    out_specs = (P("rows", "cols"), P("rows", "cols"))
    return jax.shard_map(local, mesh=mesh, in_specs=in_specs, out_specs=out_specs, check_vma=False)
```

```python
import math

import jax
import jax.numpy as jnp
from jax import lax
from jax.experimental import pallas as pl
from jax.experimental.pallas import tpu as pltpu
from jax.sharding import PartitionSpec as P


F32 = jnp.float32
BF16 = jnp.bfloat16
NN = ((1,), (0,))
NT = ((1,), (1,))
TN = ((0,), (0,))


def mm(a, b, dims, precision=None):
    return lax.dot_general(
        a, b, (dims, ((), ())), precision=precision, preferred_element_type=F32
    )


def split(a):
    high = a.astype(BF16)
    return high, (a - high.astype(F32)).astype(BF16)


def cube(inner):
    shifted = inner + 1.0
    return (shifted * shifted * shifted).astype(BF16)


def three(a):
    high = a.astype(BF16).astype(F32)
    rest = a - high
    middle = rest.astype(BF16).astype(F32)
    return high, middle, rest - middle


def factor_inverse(rows, n, jobs):
    blocks = n // 8
    lane = lax.broadcasted_iota(jnp.int32, (8, n), 1)
    sub = lax.broadcasted_iota(jnp.int32, (8, n), 0)
    rows = list(rows)
    done = []

    def row_of(a, t):
        return jnp.broadcast_to(a[t : t + 1, :], (8, n))

    for g in range(blocks):
        first = 8 * g
        inside = (lane >= first) & (lane < first + 8)
        pivot = jnp.where(inside, jnp.where(lane == sub + first, 1.0, 0.0), rows[g])
        near = min(g + 2, blocks) - g
        column = [
            [jnp.broadcast_to(rows[g + v][:, first + k : first + k + 1], (8, n)) for k in range(8)]
            for v in range(near)
        ]
        factor = [None] * 8
        diagonal = jnp.zeros((8, n), F32)
        if jobs:
            jobs.pop(0)()
        for t in range(0, 8, 2):
            c0, c1 = column[0][t], column[0][t + 1]
            a, b, d = row_of(c0, t), row_of(c1, t), row_of(c1, t + 1)
            det = a * d - b * b
            ra, rdet = 1.0 / a, 1.0 / det
            ratio = b * ra
            diagonal = jnp.where(sub == t, a, jnp.where(sub == t + 1, det * ra, diagonal))
            own0 = jnp.where(sub > t, c0 * ra, 0.0)
            own1 = jnp.where(sub > t + 1, (c1 * a - c0 * b) * rdet, 0.0)
            if near > 1:
                n0, n1 = column[1][t], column[1][t + 1]
                factor[t], factor[t + 1] = n0 * ra, (n1 * a - n0 * b) * rdet
            for k in range(t + 2, 8):
                e0 = row_of(column[0][k], t)
                e1 = row_of(column[0][k], t + 1) - ratio * e0
                column[0][k] = column[0][k] - own0 * e0 - own1 * e1
                if near > 1:
                    column[1][k] = column[1][k] - factor[t] * e0 - factor[t + 1] * e1
            p0 = row_of(pivot, t)
            p1 = row_of(pivot, t + 1) - ratio * p0
            pivot = pivot - own0 * p0 - own1 * p1
        if g + 2 < blocks:
            a1, a2, a3 = three(pivot * (1.0 / diagonal))
            b1, b2, b3 = three(pivot)
            left = jnp.concatenate([a1, a1, a2, a2, a1, a3], axis=0).astype(BF16)
            right = jnp.concatenate([b1, b2, b1, b2, b3, b1], axis=0).astype(BF16)
            update = mm(left, right, TN)
            for v in range(g + 2, blocks):
                rows[v] = jnp.where(inside, 0.0, rows[v]) - update[8 * v : 8 * v + 8, :]
        if near > 1:
            m = jnp.where(inside, 0.0, rows[g + 1])
            for t in range(8):
                m = m - factor[t] * row_of(pivot, t)
            rows[g + 1] = m
        done.append(jnp.where(lane <= sub + first, pivot, 0.0) * lax.rsqrt(diagonal))
    return jnp.concatenate(done, axis=0)


def inverse_factor(gram, jobs, base=128):
    n = gram.shape[0]
    if n <= base:
        return factor_inverse([gram[8 * i : 8 * i + 8, :] for i in range(n // 8)], n, jobs)
    k = n // 2
    high = lax.Precision.HIGHEST
    w11 = inverse_factor(gram[:k, :k], jobs, base)
    l21 = mm(gram[k:, :k], w11, NT, high)
    w22 = inverse_factor(gram[k:, k:] - mm(l21, l21, NT, high), jobs, base)
    w21 = -mm(w22, mm(l21, w11, NN, high), NN, high)
    top = jnp.concatenate([w11, jnp.zeros((k, n - k), F32)], axis=1)
    return jnp.concatenate([top, jnp.concatenate([w21, w22], axis=1)], axis=0)


def sketch_kernel(scale, quarter, x_ref, y_ref, t_ref, own_ref, *refs):
    piece_refs, (x4, total) = refs[:-2], refs[-2:]
    step = pl.program_id(0)
    c = lax.axis_index("cols")

    def first_row(bits):
        i = c ^ bits
        return pl.multiple_of((i % 2) * (total.shape[0] // 2) + (i // 2) * quarter, quarter)


    @pl.when(step == 0)
    def _():
        pairs = jnp.concatenate(split(x_ref[...] * scale), axis=0).T
        x4[...] = jnp.concatenate([pairs, pairs], axis=1)
        depth, columns = own_ref.shape
        width = x_ref.shape[0]
        packed = []
        for b in range(columns // width):
            if b * depth < quarter:
                rows = pl.ds(pl.multiple_of(first_row(0) + b * depth, depth), depth)
                packed.append(x4[rows, :][:, :width])
            else:
                packed.append(jnp.zeros((depth, width), BF16))
        own_ref[...] = jnp.concatenate(packed, axis=1)
        total[...] = jnp.zeros_like(total)

    high, low = split(y_ref[...])
    y4 = jnp.concatenate([high, high, low, low], axis=0)
    sub = 256
    for i in range(total.shape[0] // sub):
        there = slice(i * sub, (i + 1) * sub)
        total[there, :] += mm(cube(mm(x4[there, :], y4, NN)), t_ref[...], NN)

    @pl.when(step == pl.num_programs(0) - 1)
    def _():
        for bits, piece_ref in enumerate(piece_refs):
            piece_ref[...] = total[pl.ds(first_row(bits), quarter), :].astype(piece_ref.dtype)


def sketch_call(x_t, y_t, test, scale, quarter, depth):
    width, rows = x_t.shape
    cols, columns = test.shape
    tile = 2048
    whole = lambda shape: pl.BlockSpec(shape, lambda j: (0, 0))
    count = rows // quarter
    types = [F32 if bits < 2 else BF16 for bits in range(count)]
    return pl.pallas_call(
        lambda *refs: sketch_kernel(scale, quarter, *refs),
        grid=(cols // tile,),
        in_specs=[
            whole((width, rows)),
            pl.BlockSpec((width, tile), lambda j: (0, j)),
            pl.BlockSpec((tile, columns), lambda j: (j, 0)),
        ],
        out_specs=[
            whole((depth, columns)),
        ]
        + [whole((quarter, columns))] * count,
        out_shape=[jax.ShapeDtypeStruct((depth, columns), BF16)]
        + [jax.ShapeDtypeStruct((quarter, columns), t) for t in types],
        scratch_shapes=[pltpu.VMEM((rows, 4 * width), BF16), pltpu.VMEM((rows, columns), F32)],
        name="sketch_tile",
    )(x_t, y_t, test)


def columns_kernel(y_ref, y2_ref):
    cols = y2_ref.shape[0]
    start = (lax.axis_index("rows") % 2) * cols
    high, low = split(y_ref[:, pl.ds(pl.multiple_of(start, cols), cols)])
    y2_ref[...] = jnp.concatenate([high, low], axis=0).T


def columns_call(y_t):
    width, cols = y_t.shape
    return pl.pallas_call(
        columns_kernel,
        out_shape=jax.ShapeDtypeStruct((cols // 2, 2 * width), BF16),
        cost_estimate=pl.CostEstimate(
            flops=0, bytes_accessed=4 * y_t.size + 4 * width * cols, transcendentals=0
        ),
        compiler_params=pltpu.CompilerParams(vmem_limit_bytes=24 * 2**20),
        name="column_pieces",
    )(y_t)


def sketch_rows(parts, quarter, depth):
    return jnp.concatenate(
        [a[j : j + quarter, :] for a in parts for j in range(0, a.shape[0], quarter + depth)], axis=0
    )


def gram_of(sketches, total=None):
    for s in sketches:
        part = mm(s, s, TN)
        total = part if total is None else total + part
    return total


def gram_kernel(quarter, depth, count, first, *refs):
    refs, g_ref = refs[:-1], refs[-1]
    sketches = [sketch_rows([a], quarter, depth) for a in refs[:count]]
    g_ref[...] = gram_of(sketches, None if first else refs[count][...])


def gram_call(pieces, quarter, depth, carry=None):
    columns = pieces[0].shape[1]
    first = carry is None
    return pl.pallas_call(
        lambda *refs: gram_kernel(quarter, depth, len(pieces), first, *refs),
        out_shape=jax.ShapeDtypeStruct((columns, columns), F32),
        cost_estimate=pl.CostEstimate(
            flops=2 * columns * columns * sum(a.shape[0] for a in pieces),
            bytes_accessed=2 * sum(a.size for a in pieces) + 8 * columns * columns,
            transcendentals=0,
        ),
        compiler_params=pltpu.CompilerParams(vmem_limit_bytes=24 * 2**20),
        name="sketch_gram",
    )(*pieces, *(() if first else (carry,)))


def final_kernel(places, depth, early, groups, *refs):
    count = sum(groups)
    parts, refs = refs[:count], refs[count:]
    (y2_ref, g_ref), refs = refs[:2], refs[2:]
    basis_ref, projected_ref, given_ref, w, s, z, x2 = refs
    columns = g_ref.shape[0]
    cols = z.shape[0]
    width = y2_ref.shape[1] // 2
    quarter = s.shape[0] // len(places)
    for place, piece in places:
        rows = pl.ds(pl.multiple_of(place() * quarter, quarter), quarter)
        s[rows, :] = parts[piece][:quarter, :]
    sources, first = [], 0
    for n in groups:
        sources.append(parts[first : first + n])
        first += n

    def sketch(n):
        return sketch_rows(sources[n], quarter, depth)

    def features(n):
        rows = []
        for part in sources[n]:
            for j in range(quarter, part.shape[0], quarter + depth):
                packed = part[j : j + depth, :]
                for b in range(quarter // depth):
                    a = packed[:, b * width : (b + 1) * width]
                    rows.append(jnp.concatenate([a, a], axis=1))
        return jnp.concatenate(rows, axis=0)

    gram = gram_of([sketch(n) for n in range(early, len(groups))], g_ref[...])

    sub = 256
    work = [(i, n) for i in range(cols // sub) for n in range(len(groups))]
    slots = columns // 8

    def job(part):
        def run():
            for i, n in part:
                there = slice(i * sub, (i + 1) * sub)
                if i == 0:
                    x2[n] = features(n)
                term = mm(cube(mm(y2_ref[there, :], x2[n], NT)), sketch(n), NN)
                z[there, :] = term if n == 0 else z[there, :] + term

        return run

    bounds = [len(work) * i // slots for i in range(slots + 1)]
    jobs = [job(work[i:j]) for i, j in zip(bounds, bounds[1:])]
    w[...] = inverse_factor(gram, jobs)

    own_r, own_c = projected_ref.shape[0], basis_ref.shape[0]
    ir, ic = lax.axis_index("rows"), lax.axis_index("cols")

    def rows_of(i, n):
        return split(w[pl.ds(pl.multiple_of(i * n, n), n), :])

    mine, given = rows_of(ir, own_r), rows_of(ir ^ 1, own_r)
    tall = jnp.concatenate([mine[0], given[0], mine[1], given[1]], axis=0)
    start = (ir % 2) * cols
    tile = 512
    for j in range(cols // tile):
        high, low = split(z[tile * j : tile * (j + 1), :])
        both = mm(tall, high, NT)
        both = both[: 2 * own_r] + both[2 * own_r :] + mm(tall[: 2 * own_r], low, NT)
        there = pl.ds(pl.multiple_of(start + tile * j, tile), tile)
        projected_ref[:, there] = both[:own_r]
        given_ref[:, tile * j : tile * (j + 1)] = both[own_r:].astype(BF16)
    both = mm(jnp.concatenate(rows_of(ic, own_c), axis=0), s[...], NT)
    basis_ref[...] = both[:own_c] + both[own_c:]


def final_call(groups, early, y2, gram, places, quarter, depth, own_r, own_c):
    columns = gram.shape[0]
    parts = [a for group in groups for a in group]
    counts = [len(group) for group in groups]
    height = quarter * len(places)
    tall = sum(a.shape[0] for a in groups[0]) // (quarter + depth) * quarter
    cols = y2.shape[0]
    return pl.pallas_call(
        lambda *refs: final_kernel(places, depth, early, counts, *refs),
        out_shape=[
            jax.ShapeDtypeStruct((own_c, height), F32),
            jax.ShapeDtypeStruct((own_r, 2 * cols), F32),
            jax.ShapeDtypeStruct((own_r, cols), BF16),
        ],
        scratch_shapes=[
            pltpu.VMEM((columns, columns), F32),
            pltpu.VMEM((height, columns), BF16),
            pltpu.VMEM((cols, columns), F32),
            pltpu.VMEM((len(groups), tall, y2.shape[1]), BF16),
        ],
        compiler_params=pltpu.CompilerParams(vmem_limit_bytes=40 * 2**20),
        name="factor_and_project",
    )(*parts, y2, gram)


def swap(a, axis, bits):
    return lax.ppermute(a, axis, [(i, i ^ bits) for i in range(lax.axis_size(axis))])


def local(row_features, col_features, test_block):
    cols = lax.axis_size("cols")
    rows = lax.axis_size("rows")
    chips_y, chips_z = cols // 2, rows // 2
    ir = lax.axis_index("rows")
    height, width = row_features.shape
    scale = 1.0 / math.sqrt(width)
    columns = test_block.shape[1]
    half = height // 2
    quarter = half // chips_y

    x_t, y_t = row_features.T, col_features.T
    depth = max(16, quarter * width // columns)
    x_own, s_own, *given = sketch_call(x_t, y_t, test_block, scale, quarter, depth)
    y2 = columns_call(y_t)
    for bits, a in list(enumerate(given, 1))[::-1]:
        s_own = s_own + swap(a, "cols", bits).astype(F32)
    piece = jnp.concatenate([s_own.astype(BF16), x_own], axis=0)

    along_z = {0: piece}
    for d in range(1, chips_z):
        along_z[d] = swap(piece, "rows", 2 * d)
    own = jnp.concatenate([along_z[d] for d in range(chips_z)], 0)
    near_x = swap(own, "rows", 1)
    near_y = [swap(own, "cols", 2 * d) for d in range(1, chips_y)]
    own_core = swap(own, "cols", 1)
    gram = gram_call([own, own_core], quarter, depth)
    cut = own.shape[0] // 2
    far = []
    for d in range(1, chips_y):
        low = swap(near_y[d - 1][:cut], "rows", 1)
        far.append([low, swap(near_x[cut:], "cols", 2 * d)])
    near = [near_x] + near_y
    near_core = [swap(a, "cols", 1) for a in near]
    gram = gram_call(near + near_core, quarter, depth, gram)
    singles = [own, own_core] + near + near_core
    early = len(singles)
    groups = [[a] for a in singles] + far + [[swap(a, "cols", 1) for a in pair] for pair in far]

    places = []
    with_y = len(near)
    for k, group in enumerate(
        (
            [0] + list(range(3, 2 + with_y)),
            [1] + list(range(3 + with_y, 2 + 2 * with_y)),
        )
    ):
        for d, n in enumerate(group):

            def place(k=k, d=d):
                c = lax.axis_index("cols")
                return ((c % 2) ^ k) * chips_y + ((c // 2) ^ d)

            places.append((place, n))
    basis_t, projected, given = final_call(
        groups, early, y2, gram, places, quarter, depth, columns // rows, columns // cols
    )
    there = swap(given, "rows", 1).astype(F32)
    projected = lax.dynamic_update_slice_in_dim(
        projected, there, (1 - ir % 2) * there.shape[1], 1
    )
    return (basis_t.T, projected)


def solution(mesh):
    in_specs = (P("rows", None), P("cols", None), P("cols", None))
    out_specs = (P("rows", "cols"), P("rows", "cols"))
    return jax.shard_map(local, mesh=mesh, in_specs=in_specs, out_specs=out_specs, check_vma=False)
```

```python
import math

import jax
import jax.numpy as jnp
from jax import lax
from jax.experimental import pallas as pl
from jax.experimental.pallas import tpu as pltpu
from jax.sharding import PartitionSpec as P


F32 = jnp.float32
BF16 = jnp.bfloat16
NN = ((1,), (0,))
NT = ((1,), (1,))
TN = ((0,), (0,))


def mm(a, b, dims, precision=None):
    return lax.dot_general(
        a, b, (dims, ((), ())), precision=precision, preferred_element_type=F32
    )


def split(a):
    high = a.astype(BF16)
    return high, (a - high.astype(F32)).astype(BF16)


def cube(inner):
    shifted = inner + 1.0
    return (shifted * shifted * shifted).astype(BF16)


def three(a):
    high = a.astype(BF16).astype(F32)
    rest = a - high
    middle = rest.astype(BF16).astype(F32)
    return high, middle, rest - middle


def factor_inverse(rows, n, jobs):
    blocks = n // 8
    lane = lax.broadcasted_iota(jnp.int32, (8, n), 1)
    sub = lax.broadcasted_iota(jnp.int32, (8, n), 0)
    rows = list(rows)
    done = []

    def row_of(a, t):
        return jnp.broadcast_to(a[t : t + 1, :], (8, n))

    for g in range(blocks):
        first = 8 * g
        inside = (lane >= first) & (lane < first + 8)
        pivot = jnp.where(inside, jnp.where(lane == sub + first, 1.0, 0.0), rows[g])
        near = min(g + 3, blocks) - g
        column = [
            [jnp.broadcast_to(rows[g + v][:, first + k : first + k + 1], (8, n)) for k in range(8)]
            for v in range(near)
        ]
        factor = [[None] * 8 for _ in range(near)]
        diagonal = jnp.zeros((8, n), F32)
        if jobs:
            jobs.pop(0)()
        for t in range(0, 8, 2):
            c0, c1 = column[0][t], column[0][t + 1]
            a, b, d = row_of(c0, t), row_of(c1, t), row_of(c1, t + 1)
            det = a * d - b * b
            ra, rdet = 1.0 / a, 1.0 / det
            ratio = b * ra
            diagonal = jnp.where(sub == t, a, jnp.where(sub == t + 1, det * ra, diagonal))
            own0 = jnp.where(sub > t, c0 * ra, 0.0)
            own1 = jnp.where(sub > t + 1, (c1 * a - c0 * b) * rdet, 0.0)
            for v in range(1, near):
                n0, n1 = column[v][t], column[v][t + 1]
                factor[v][t], factor[v][t + 1] = n0 * ra, (n1 * a - n0 * b) * rdet
            for k in range(t + 2, 8):
                e0 = row_of(column[0][k], t)
                e1 = row_of(column[0][k], t + 1) - ratio * e0
                column[0][k] = column[0][k] - own0 * e0 - own1 * e1
                for v in range(1, near):
                    column[v][k] = column[v][k] - factor[v][t] * e0 - factor[v][t + 1] * e1
            p0 = row_of(pivot, t)
            p1 = row_of(pivot, t + 1) - ratio * p0
            pivot = pivot - own0 * p0 - own1 * p1
        if g + 3 < blocks:
            a1, a2, a3 = three(pivot * (1.0 / diagonal))
            b1, b2, b3 = three(pivot)
            left = jnp.concatenate([a1, a1, a2, a2, a1, a3], axis=0).astype(BF16)
            right = jnp.concatenate([b1, b2, b1, b2, b3, b1], axis=0).astype(BF16)
            update = mm(left, right, TN)
            for v in range(g + 3, blocks):
                rows[v] = jnp.where(inside, 0.0, rows[v]) - update[8 * v : 8 * v + 8, :]
        pivots = [row_of(pivot, t) for t in range(8)]
        for v in range(1, near):
            m = jnp.where(inside, 0.0, rows[g + v])
            for t in range(8):
                m = m - factor[v][t] * pivots[t]
            rows[g + v] = m
        done.append(jnp.where(lane <= sub + first, pivot, 0.0) * lax.rsqrt(diagonal))
    return jnp.concatenate(done, axis=0)


def inverse_factor(gram, jobs, base=128):
    n = gram.shape[0]
    if n <= base:
        return factor_inverse([gram[8 * i : 8 * i + 8, :] for i in range(n // 8)], n, jobs)
    k = n // 2
    high = lax.Precision.HIGHEST
    w11 = inverse_factor(gram[:k, :k], jobs, base)
    l21 = mm(gram[k:, :k], w11, NT, high)
    w22 = inverse_factor(gram[k:, k:] - mm(l21, l21, NT, high), jobs, base)
    w21 = -mm(w22, mm(l21, w11, NN, high), NN, high)
    top = jnp.concatenate([w11, jnp.zeros((k, n - k), F32)], axis=1)
    return jnp.concatenate([top, jnp.concatenate([w21, w22], axis=1)], axis=0)


def sketch_kernel(scale, quarter, x_ref, y_ref, t_ref, own_ref, *refs):
    piece_refs, (x4, total) = refs[:-2], refs[-2:]
    step = pl.program_id(0)
    c = lax.axis_index("cols")

    def first_row(bits):
        i = c ^ bits
        return pl.multiple_of((i % 2) * (total.shape[0] // 2) + (i // 2) * quarter, quarter)


    @pl.when(step == 0)
    def _():
        pairs = jnp.concatenate(split(x_ref[...] * scale), axis=0).T
        x4[...] = jnp.concatenate([pairs, pairs], axis=1)
        depth, columns = own_ref.shape
        width = x_ref.shape[0]
        packed = []
        for b in range(columns // width):
            if b * depth < quarter:
                rows = pl.ds(pl.multiple_of(first_row(0) + b * depth, depth), depth)
                packed.append(x4[rows, :][:, :width])
            else:
                packed.append(jnp.zeros((depth, width), BF16))
        own_ref[...] = jnp.concatenate(packed, axis=1)
        total[...] = jnp.zeros_like(total)

    high, low = split(y_ref[...])
    y4 = jnp.concatenate([high, high, low, low], axis=0)
    sub = 256
    for i in range(total.shape[0] // sub):
        there = slice(i * sub, (i + 1) * sub)
        total[there, :] += mm(cube(mm(x4[there, :], y4, NN)), t_ref[...], NN)

    @pl.when(step == pl.num_programs(0) - 1)
    def _():
        for bits, piece_ref in enumerate(piece_refs):
            piece_ref[...] = total[pl.ds(first_row(bits), quarter), :].astype(piece_ref.dtype)


def sketch_call(x_t, y_t, test, scale, quarter, depth):
    width, rows = x_t.shape
    cols, columns = test.shape
    tile = 2048
    whole = lambda shape: pl.BlockSpec(shape, lambda j: (0, 0))
    count = rows // quarter
    types = [F32 if bits < 2 else BF16 for bits in range(count)]
    return pl.pallas_call(
        lambda *refs: sketch_kernel(scale, quarter, *refs),
        grid=(cols // tile,),
        in_specs=[
            whole((width, rows)),
            pl.BlockSpec((width, tile), lambda j: (0, j)),
            pl.BlockSpec((tile, columns), lambda j: (j, 0)),
        ],
        out_specs=[
            whole((depth, columns)),
        ]
        + [whole((quarter, columns))] * count,
        out_shape=[jax.ShapeDtypeStruct((depth, columns), BF16)]
        + [jax.ShapeDtypeStruct((quarter, columns), t) for t in types],
        scratch_shapes=[pltpu.VMEM((rows, 4 * width), BF16), pltpu.VMEM((rows, columns), F32)],
        name="sketch_tile",
    )(x_t, y_t, test)


def columns_kernel(y_ref, y2_ref):
    cols = y2_ref.shape[0]
    start = (lax.axis_index("rows") % 2) * cols
    high, low = split(y_ref[:, pl.ds(pl.multiple_of(start, cols), cols)])
    y2_ref[...] = jnp.concatenate([high, low], axis=0).T


def columns_call(y_t):
    width, cols = y_t.shape
    return pl.pallas_call(
        columns_kernel,
        out_shape=jax.ShapeDtypeStruct((cols // 2, 2 * width), BF16),
        cost_estimate=pl.CostEstimate(
            flops=0, bytes_accessed=4 * y_t.size + 4 * width * cols, transcendentals=0
        ),
        compiler_params=pltpu.CompilerParams(vmem_limit_bytes=24 * 2**20),
        name="column_pieces",
    )(y_t)


def sketch_rows(parts, quarter, depth):
    return jnp.concatenate(
        [a[j : j + quarter, :] for a in parts for j in range(0, a.shape[0], quarter + depth)], axis=0
    )


def feature_rows(parts, quarter, depth, width):
    rows = []
    for part in parts:
        for j in range(quarter, part.shape[0], quarter + depth):
            packed = part[j : j + depth, :]
            for b in range(quarter // depth):
                a = packed[:, b * width : (b + 1) * width]
                rows.append(jnp.concatenate([a, a], axis=1))
    return jnp.concatenate(rows, axis=0)


def product_kernel(quarter, depth, count, first, *refs):
    pieces, y2_ref, z_ref = refs[:count], refs[count], refs[-1]
    width = y2_ref.shape[1] // 2
    sub = 256
    for a in pieces:
        x2, s = feature_rows([a], quarter, depth, width), sketch_rows([a], quarter, depth)
        for i in range(z_ref.shape[0] // sub):
            there = slice(i * sub, (i + 1) * sub)
            term = mm(cube(mm(y2_ref[there, :], x2, NT)), s, NN)
            if a is pieces[0]:
                z_ref[there, :] = term if first else refs[-2][there, :] + term
            else:
                z_ref[there, :] += term


def product_call(pieces, y2, quarter, depth, carry=None):
    first = carry is None
    cols, columns = y2.shape[0], pieces[0].shape[1]
    rows = sum(a.shape[0] for a in pieces)
    return pl.pallas_call(
        lambda *refs: product_kernel(quarter, depth, len(pieces), first, *refs),
        out_shape=jax.ShapeDtypeStruct((cols, columns), F32),
        input_output_aliases={} if first else {len(pieces) + 1: 0},
        cost_estimate=pl.CostEstimate(
            flops=4 * cols * rows * columns,
            bytes_accessed=2 * (rows * columns + y2.size) + 4 * cols * columns,
            transcendentals=0,
        ),
        compiler_params=pltpu.CompilerParams(vmem_limit_bytes=32 * 2**20),
        name="kernel_times_sketch",
    )(*pieces, y2, *(() if first else (carry,)))


def hold_kernel(x_ref, s_ref, x_out, s_out):
    x_out[...] = x_ref[...]
    s_out[...] = s_ref[...]


def hold_call(x_own, s_own):
    return pl.pallas_call(
        hold_kernel,
        out_shape=[jax.ShapeDtypeStruct(a.shape, a.dtype) for a in (x_own, s_own)],
        compiler_params=pltpu.CompilerParams(vmem_limit_bytes=16 * 2**20),
        name="hold_own",
    )(x_own, s_own)


def piece_kernel(x_ref, *refs):
    out_ref = refs[-1]
    total = refs[0][...]
    for a in refs[1:-1]:
        total = total + a[...].astype(F32)
    out_ref[: total.shape[0], :] = total.astype(BF16)
    out_ref[total.shape[0] :, :] = x_ref[...]


def piece_call(x_own, terms):
    shape = (terms[0].shape[0] + x_own.shape[0], x_own.shape[1])
    return pl.pallas_call(
        piece_kernel,
        out_shape=jax.ShapeDtypeStruct(shape, BF16),
        compiler_params=pltpu.CompilerParams(vmem_limit_bytes=16 * 2**20),
        name="own_piece",
    )(x_own, *terms)


def gram_of(sketches, total=None):
    for s in sketches:
        part = mm(s, s, TN)
        total = part if total is None else total + part
    return total


def gram_kernel(quarter, depth, count, first, *refs):
    refs, g_ref = refs[:-1], refs[-1]
    sketches = [sketch_rows([a], quarter, depth) for a in refs[:count]]
    g_ref[...] = gram_of(sketches, None if first else refs[count][...])


def gram_call(pieces, quarter, depth, carry=None):
    columns = pieces[0].shape[1]
    first = carry is None
    return pl.pallas_call(
        lambda *refs: gram_kernel(quarter, depth, len(pieces), first, *refs),
        out_shape=jax.ShapeDtypeStruct((columns, columns), F32),
        cost_estimate=pl.CostEstimate(
            flops=2 * columns * columns * sum(a.shape[0] for a in pieces),
            bytes_accessed=2 * sum(a.size for a in pieces) + 8 * columns * columns,
            transcendentals=0,
        ),
        compiler_params=pltpu.CompilerParams(vmem_limit_bytes=24 * 2**20),
        name="sketch_gram",
    )(*pieces, *(() if first else (carry,)))


def final_kernel(places, depth, done, early, groups, *refs):
    count = sum(groups)
    parts, refs = refs[:count], refs[count:]
    (y2_ref, g_ref, z_in), refs = refs[:3], refs[3:]
    basis_ref, projected_ref, given_ref, w, s, z, x2 = refs
    columns = g_ref.shape[0]
    cols = z.shape[0]
    width = y2_ref.shape[1] // 2
    quarter = s.shape[0] // len(places)
    for place, piece in places:
        rows = pl.ds(pl.multiple_of(place() * quarter, quarter), quarter)
        s[rows, :] = parts[piece][:quarter, :]
    sources, first = [], 0
    for n in groups:
        sources.append(parts[first : first + n])
        first += n

    def sketch(n):
        return sketch_rows(sources[n], quarter, depth)

    def features(n):
        return feature_rows(sources[n], quarter, depth, width)

    gram = gram_of([sketch(n) for n in range(early, len(groups))], g_ref[...])

    sub = 256
    work = [(i, n) for i in range(cols // sub) for n in range(done, len(groups))]
    slots = columns // 8

    def job(part):
        def run():
            for i, n in part:
                there = slice(i * sub, (i + 1) * sub)
                if i == 0:
                    x2[n - done] = features(n)
                term = mm(cube(mm(y2_ref[there, :], x2[n - done], NT)), sketch(n), NN)
                z[there, :] = term + (z_in if n == done else z)[there, :]

        return run

    bounds = [len(work) * i // slots for i in range(slots + 1)]
    jobs = [job(work[i:j]) for i, j in zip(bounds, bounds[1:])]
    w[...] = inverse_factor(gram, jobs)

    own_r, own_c = projected_ref.shape[0], basis_ref.shape[0]
    ir, ic = lax.axis_index("rows"), lax.axis_index("cols")

    def rows_of(i, n):
        return split(w[pl.ds(pl.multiple_of(i * n, n), n), :])

    mine, given = rows_of(ir, own_r), rows_of(ir ^ 1, own_r)
    tall = jnp.concatenate([mine[0], given[0], mine[1], given[1]], axis=0)
    tile = 512
    for j in range(cols // tile):
        high, low = split(z[tile * j : tile * (j + 1), :])
        both = mm(tall, high, NT)
        both = both[: 2 * own_r] + both[2 * own_r :] + mm(tall[: 2 * own_r], low, NT)
        there = slice(tile * j, tile * (j + 1))
        projected_ref[:, there] = both[:own_r]
        given_ref[:, there] = both[own_r:].astype(BF16)
    both = mm(jnp.concatenate(rows_of(ic, own_c), axis=0), s[...], NT)
    basis_ref[...] = both[:own_c] + both[own_c:]


def final_call(groups, done, early, y2, gram, z, places, quarter, depth, own_r, own_c):
    columns = gram.shape[0]
    parts = [a for group in groups for a in group]
    counts = [len(group) for group in groups]
    height = quarter * len(places)
    tall = sum(a.shape[0] for a in groups[0]) // (quarter + depth) * quarter
    cols = y2.shape[0]
    return pl.pallas_call(
        lambda *refs: final_kernel(places, depth, done, early, counts, *refs),
        out_shape=[
            jax.ShapeDtypeStruct((own_c, height), F32),
            jax.ShapeDtypeStruct((own_r, cols), F32),
            jax.ShapeDtypeStruct((own_r, cols), BF16),
        ],
        scratch_shapes=[
            pltpu.VMEM((columns, columns), F32),
            pltpu.VMEM((height, columns), BF16),
            pltpu.VMEM((cols, columns), F32),
            pltpu.VMEM((len(groups) - done, tall, y2.shape[1]), BF16),
        ],
        compiler_params=pltpu.CompilerParams(vmem_limit_bytes=40 * 2**20),
        name="factor_and_project",
    )(*parts, y2, gram, z)


def assemble_kernel(mine_ref, there_ref, out_ref):
    cols = mine_ref.shape[1]
    near = lax.axis_index("rows") % 2
    out_ref[:, pl.ds(pl.multiple_of(near * cols, cols), cols)] = mine_ref[...]
    out_ref[:, pl.ds(pl.multiple_of((1 - near) * cols, cols), cols)] = there_ref[...].astype(F32)


def assemble_call(mine, there):
    rows, cols = mine.shape
    return pl.pallas_call(
        assemble_kernel,
        out_shape=jax.ShapeDtypeStruct((rows, 2 * cols), F32),
        compiler_params=pltpu.CompilerParams(vmem_limit_bytes=16 * 2**20),
        name="both_halves",
    )(mine, there)


def swap(a, axis, bits):
    return lax.ppermute(a, axis, [(i, i ^ bits) for i in range(lax.axis_size(axis))])


def local(row_features, col_features, test_block):
    cols = lax.axis_size("cols")
    rows = lax.axis_size("rows")
    chips_y, chips_z = cols // 2, rows // 2
    height, width = row_features.shape
    scale = 1.0 / math.sqrt(width)
    columns = test_block.shape[1]
    half = height // 2
    quarter = half // chips_y

    x_t, y_t = row_features.T, col_features.T
    depth = max(16, quarter * width // columns)
    x_own, s_own, *given = sketch_call(x_t, y_t, test_block, scale, quarter, depth)
    y2 = columns_call(y_t)
    there = [swap(a, "cols", bits) for bits, a in list(enumerate(given, 1))[::-1]]
    x_own, s_own = hold_call(x_own, s_own)
    piece = piece_call(x_own, [s_own] + there)

    along_z = {0: piece}
    for d in range(1, chips_z):
        along_z[d] = swap(piece, "rows", 2 * d)
    own = jnp.concatenate([along_z[d] for d in range(chips_z)], 0)
    near_x = swap(own, "rows", 1)
    near_y = [swap(own, "cols", 2 * d) for d in range(1, chips_y)]
    own_core = swap(own, "cols", 1)
    gram = gram_call([own, own_core], quarter, depth)
    z = product_call([own], y2, quarter, depth)
    z = product_call([own_core], y2, quarter, depth, z)
    cut = own.shape[0] // 2
    far = []
    for d in range(1, chips_y):
        low = swap(near_y[d - 1][:cut], "rows", 1)
        far.append([low, swap(near_x[cut:], "cols", 2 * d)])
    near = [near_x] + near_y
    near_core = [swap(a, "cols", 1) for a in near]
    gram = gram_call(near + near_core, quarter, depth, gram)
    z = product_call(near, y2, quarter, depth, z)
    singles = [own, own_core] + near + near_core
    done = 2 + len(near)
    early = len(singles)
    groups = [[a] for a in singles] + far + [[swap(a, "cols", 1) for a in pair] for pair in far]

    places = []
    with_y = len(near)
    for k, group in enumerate(
        (
            [0] + list(range(3, 2 + with_y)),
            [1] + list(range(3 + with_y, 2 + 2 * with_y)),
        )
    ):
        for d, n in enumerate(group):

            def place(k=k, d=d):
                c = lax.axis_index("cols")
                return ((c % 2) ^ k) * chips_y + ((c // 2) ^ d)

            places.append((place, n))
    basis_t, projected, given = final_call(
        groups, done, early, y2, gram, z, places, quarter, depth, columns // rows, columns // cols
    )
    projected = assemble_call(projected, swap(given, "rows", 1))
    return (basis_t.T, projected)


def solution(mesh):
    in_specs = (P("rows", None), P("cols", None), P("cols", None))
    out_specs = (P("rows", "cols"), P("rows", "cols"))
    return jax.shard_map(local, mesh=mesh, in_specs=in_specs, out_specs=out_specs, check_vma=False)
```

```python
import math

import jax
import jax.numpy as jnp
from jax import lax
from jax.experimental import pallas as pl
from jax.experimental.pallas import tpu as pltpu
from jax.sharding import PartitionSpec as P


F32 = jnp.float32
BF16 = jnp.bfloat16
NN = ((1,), (0,))
NT = ((1,), (1,))
TN = ((0,), (0,))


def mm(a, b, dims, precision=None):
    return lax.dot_general(
        a, b, (dims, ((), ())), precision=precision, preferred_element_type=F32
    )


def split(a):
    high = a.astype(BF16)
    return high, (a - high.astype(F32)).astype(BF16)


def cube(inner):
    shifted = inner + 1.0
    return (shifted * shifted * shifted).astype(BF16)


def three(a):
    high = a.astype(BF16).astype(F32)
    rest = a - high
    middle = rest.astype(BF16).astype(F32)
    return high, middle, rest - middle


def factor_inverse(rows, n, jobs):
    blocks = n // 8
    lane = lax.broadcasted_iota(jnp.int32, (8, n), 1)
    sub = lax.broadcasted_iota(jnp.int32, (8, n), 0)
    rows = list(rows)
    done = []

    def row_of(a, t):
        return jnp.broadcast_to(a[t : t + 1, :], (8, n))

    for g in range(blocks):
        first = 8 * g
        inside = (lane >= first) & (lane < first + 8)
        pivot = jnp.where(inside, jnp.where(lane == sub + first, 1.0, 0.0), rows[g])
        near = min(g + 2, blocks) - g
        column = [
            [jnp.broadcast_to(rows[g + v][:, first + k : first + k + 1], (8, n)) for k in range(8)]
            for v in range(near)
        ]
        factor = [None] * 8
        diagonal = jnp.zeros((8, n), F32)
        if jobs:
            jobs.pop(0)()
        for t in range(0, 8, 2):
            c0, c1 = column[0][t], column[0][t + 1]
            a, b, d = row_of(c0, t), row_of(c1, t), row_of(c1, t + 1)
            det = a * d - b * b
            ra, rdet = 1.0 / a, 1.0 / det
            ratio = b * ra
            diagonal = jnp.where(sub == t, a, jnp.where(sub == t + 1, det * ra, diagonal))
            own0 = jnp.where(sub > t, c0 * ra, 0.0)
            own1 = jnp.where(sub > t + 1, (c1 * a - c0 * b) * rdet, 0.0)
            if near > 1:
                n0, n1 = column[1][t], column[1][t + 1]
                factor[t], factor[t + 1] = n0 * ra, (n1 * a - n0 * b) * rdet
            for k in range(t + 2, 8):
                e0 = row_of(column[0][k], t)
                e1 = row_of(column[0][k], t + 1) - ratio * e0
                column[0][k] = column[0][k] - own0 * e0 - own1 * e1
                if near > 1:
                    column[1][k] = column[1][k] - factor[t] * e0 - factor[t + 1] * e1
            p0 = row_of(pivot, t)
            p1 = row_of(pivot, t + 1) - ratio * p0
            pivot = pivot - own0 * p0 - own1 * p1
        if g + 2 < blocks:
            a1, a2, a3 = three(pivot * (1.0 / diagonal))
            b1, b2, b3 = three(pivot)
            left = jnp.concatenate([a1, a1, a2, a2, a1, a3], axis=0).astype(BF16)
            right = jnp.concatenate([b1, b2, b1, b2, b3, b1], axis=0).astype(BF16)
            update = mm(left, right, TN)
            for v in range(g + 2, blocks):
                rows[v] = jnp.where(inside, 0.0, rows[v]) - update[8 * v : 8 * v + 8, :]
        if near > 1:
            m = jnp.where(inside, 0.0, rows[g + 1])
            for t in range(8):
                m = m - factor[t] * row_of(pivot, t)
            rows[g + 1] = m
        done.append(jnp.where(lane <= sub + first, pivot, 0.0) * lax.rsqrt(diagonal))
    return jnp.concatenate(done, axis=0)


def inverse_factor(gram, jobs, base=128):
    n = gram.shape[0]
    if n <= base:
        return factor_inverse([gram[8 * i : 8 * i + 8, :] for i in range(n // 8)], n, jobs)
    k = n // 2
    high = lax.Precision.HIGHEST
    w11 = inverse_factor(gram[:k, :k], jobs, base)
    l21 = mm(gram[k:, :k], w11, NT, high)
    w22 = inverse_factor(gram[k:, k:] - mm(l21, l21, NT, high), jobs, base)
    w21 = -mm(w22, mm(l21, w11, NN, high), NN, high)
    top = jnp.concatenate([w11, jnp.zeros((k, n - k), F32)], axis=1)
    return jnp.concatenate([top, jnp.concatenate([w21, w22], axis=1)], axis=0)


def sketch_kernel(scale, quarter, x_ref, y_ref, t_ref, own_ref, *refs):
    piece_refs, (x4, total) = refs[:-2], refs[-2:]
    step = pl.program_id(0)
    c = lax.axis_index("cols")

    def first_row(bits):
        i = c ^ bits
        return pl.multiple_of((i % 2) * (total.shape[0] // 2) + (i // 2) * quarter, quarter)


    @pl.when(step == 0)
    def _():
        pairs = jnp.concatenate(split(x_ref[...] * scale), axis=0).T
        x4[...] = jnp.concatenate([pairs, pairs], axis=1)
        depth, columns = own_ref.shape
        width = x_ref.shape[0]
        packed = []
        for b in range(columns // width):
            if b * depth < quarter:
                rows = pl.ds(pl.multiple_of(first_row(0) + b * depth, depth), depth)
                packed.append(x4[rows, :][:, :width])
            else:
                packed.append(jnp.zeros((depth, width), BF16))
        own_ref[...] = jnp.concatenate(packed, axis=1)
        total[...] = jnp.zeros_like(total)

    high, low = split(y_ref[...])
    y4 = jnp.concatenate([high, high, low, low], axis=0)
    sub = 256
    for i in range(total.shape[0] // sub):
        there = slice(i * sub, (i + 1) * sub)
        total[there, :] += mm(cube(mm(x4[there, :], y4, NN)), t_ref[...], NN)

    @pl.when(step == pl.num_programs(0) - 1)
    def _():
        for bits, piece_ref in enumerate(piece_refs):
            piece_ref[...] = total[pl.ds(first_row(bits), quarter), :].astype(piece_ref.dtype)


def sketch_call(x_t, y_t, test, scale, quarter, depth):
    width, rows = x_t.shape
    cols, columns = test.shape
    tile = 2048
    whole = lambda shape: pl.BlockSpec(shape, lambda j: (0, 0))
    count = rows // quarter
    types = [F32 if bits < 2 else BF16 for bits in range(count)]
    return pl.pallas_call(
        lambda *refs: sketch_kernel(scale, quarter, *refs),
        grid=(cols // tile,),
        in_specs=[
            whole((width, rows)),
            pl.BlockSpec((width, tile), lambda j: (0, j)),
            pl.BlockSpec((tile, columns), lambda j: (j, 0)),
        ],
        out_specs=[
            whole((depth, columns)),
        ]
        + [whole((quarter, columns))] * count,
        out_shape=[jax.ShapeDtypeStruct((depth, columns), BF16)]
        + [jax.ShapeDtypeStruct((quarter, columns), t) for t in types],
        scratch_shapes=[pltpu.VMEM((rows, 4 * width), BF16), pltpu.VMEM((rows, columns), F32)],
        name="sketch_tile",
    )(x_t, y_t, test)


def columns_kernel(y_ref, y2_ref):
    cols = y2_ref.shape[0]
    start = (lax.axis_index("rows") % 2) * cols
    high, low = split(y_ref[:, pl.ds(pl.multiple_of(start, cols), cols)])
    y2_ref[...] = jnp.concatenate([high, low], axis=0).T


def columns_call(y_t):
    width, cols = y_t.shape
    return pl.pallas_call(
        columns_kernel,
        out_shape=jax.ShapeDtypeStruct((cols // 2, 2 * width), BF16),
        cost_estimate=pl.CostEstimate(
            flops=0, bytes_accessed=4 * y_t.size + 4 * width * cols, transcendentals=0
        ),
        compiler_params=pltpu.CompilerParams(vmem_limit_bytes=24 * 2**20),
        name="column_pieces",
    )(y_t)


def sketch_rows(parts, quarter, depth):
    return jnp.concatenate(
        [a[j : j + quarter, :] for a in parts for j in range(0, a.shape[0], quarter + depth)], axis=0
    )


def feature_rows(parts, quarter, depth, width):
    rows = []
    for part in parts:
        for j in range(quarter, part.shape[0], quarter + depth):
            packed = part[j : j + depth, :]
            for b in range(quarter // depth):
                a = packed[:, b * width : (b + 1) * width]
                rows.append(jnp.concatenate([a, a], axis=1))
    return jnp.concatenate(rows, axis=0)


def product_kernel(quarter, depth, count, first, *refs):
    pieces, y2_ref, z_ref = refs[:count], refs[count], refs[-1]
    width = y2_ref.shape[1] // 2
    sub = 256
    for a in pieces:
        x2, s = feature_rows([a], quarter, depth, width), sketch_rows([a], quarter, depth)
        for i in range(z_ref.shape[0] // sub):
            there = slice(i * sub, (i + 1) * sub)
            term = mm(cube(mm(y2_ref[there, :], x2, NT)), s, NN)
            if a is pieces[0]:
                z_ref[there, :] = term if first else refs[-2][there, :] + term
            else:
                z_ref[there, :] += term


def product_call(pieces, y2, quarter, depth, carry=None):
    first = carry is None
    cols, columns = y2.shape[0], pieces[0].shape[1]
    rows = sum(a.shape[0] for a in pieces)
    return pl.pallas_call(
        lambda *refs: product_kernel(quarter, depth, len(pieces), first, *refs),
        out_shape=jax.ShapeDtypeStruct((cols, columns), F32),
        input_output_aliases={} if first else {len(pieces) + 1: 0},
        cost_estimate=pl.CostEstimate(
            flops=4 * cols * rows * columns,
            bytes_accessed=2 * (rows * columns + y2.size) + 4 * cols * columns,
            transcendentals=0,
        ),
        compiler_params=pltpu.CompilerParams(vmem_limit_bytes=32 * 2**20),
        name="kernel_times_sketch",
    )(*pieces, y2, *(() if first else (carry,)))


def hold_kernel(x_ref, s_ref, x_out, s_out):
    x_out[...] = x_ref[...]
    s_out[...] = s_ref[...]


def hold_call(x_own, s_own):
    return pl.pallas_call(
        hold_kernel,
        out_shape=[jax.ShapeDtypeStruct(a.shape, a.dtype) for a in (x_own, s_own)],
        compiler_params=pltpu.CompilerParams(vmem_limit_bytes=16 * 2**20),
        name="hold_own",
    )(x_own, s_own)


def piece_kernel(x_ref, *refs):
    out_ref = refs[-1]
    total = refs[0][...]
    for a in refs[1:-1]:
        total = total + a[...].astype(F32)
    out_ref[: total.shape[0], :] = total.astype(BF16)
    out_ref[total.shape[0] :, :] = x_ref[...]


def piece_call(x_own, terms):
    shape = (terms[0].shape[0] + x_own.shape[0], x_own.shape[1])
    return pl.pallas_call(
        piece_kernel,
        out_shape=jax.ShapeDtypeStruct(shape, BF16),
        compiler_params=pltpu.CompilerParams(vmem_limit_bytes=16 * 2**20),
        name="own_piece",
    )(x_own, *terms)


def gram_of(sketches, total=None):
    for s in sketches:
        part = mm(s, s, TN)
        total = part if total is None else total + part
    return total


def gram_kernel(quarter, depth, count, first, *refs):
    refs, g_ref = refs[:-1], refs[-1]
    sketches = [sketch_rows([a], quarter, depth) for a in refs[:count]]
    g_ref[...] = gram_of(sketches, None if first else refs[count][...])


def gram_call(pieces, quarter, depth, carry=None):
    columns = pieces[0].shape[1]
    first = carry is None
    return pl.pallas_call(
        lambda *refs: gram_kernel(quarter, depth, len(pieces), first, *refs),
        out_shape=jax.ShapeDtypeStruct((columns, columns), F32),
        cost_estimate=pl.CostEstimate(
            flops=2 * columns * columns * sum(a.shape[0] for a in pieces),
            bytes_accessed=2 * sum(a.size for a in pieces) + 8 * columns * columns,
            transcendentals=0,
        ),
        compiler_params=pltpu.CompilerParams(vmem_limit_bytes=24 * 2**20),
        name="sketch_gram",
    )(*pieces, *(() if first else (carry,)))


def final_kernel(places, depth, done, early, groups, *refs):
    count = sum(groups)
    parts, refs = refs[:count], refs[count:]
    (y2_ref, g_ref, z_in), refs = refs[:3], refs[3:]
    basis_ref, projected_ref, given_ref, w, s, z, x2 = refs
    columns = g_ref.shape[0]
    cols = z.shape[0]
    width = y2_ref.shape[1] // 2
    quarter = s.shape[0] // len(places)
    for place, piece in places:
        rows = pl.ds(pl.multiple_of(place() * quarter, quarter), quarter)
        s[rows, :] = parts[piece][:quarter, :]
    sources, first = [], 0
    for n in groups:
        sources.append(parts[first : first + n])
        first += n

    def sketch(n):
        return sketch_rows(sources[n], quarter, depth)

    def features(n):
        return feature_rows(sources[n], quarter, depth, width)

    gram = gram_of([sketch(n) for n in range(early, len(groups))], g_ref[...])

    sub = 256
    work = [(i, n) for i in range(cols // sub) for n in range(done, len(groups))]
    slots = columns // 8

    def job(part):
        def run():
            for i, n in part:
                there = slice(i * sub, (i + 1) * sub)
                if i == 0:
                    x2[n - done] = features(n)
                term = mm(cube(mm(y2_ref[there, :], x2[n - done], NT)), sketch(n), NN)
                z[there, :] = term + (z_in if n == done else z)[there, :]

        return run

    bounds = [len(work) * i // slots for i in range(slots + 1)]
    jobs = [job(work[i:j]) for i, j in zip(bounds, bounds[1:])]
    w[...] = inverse_factor(gram, jobs)

    own_r, own_c = projected_ref.shape[0], basis_ref.shape[0]
    ir, ic = lax.axis_index("rows"), lax.axis_index("cols")

    def rows_of(i, n):
        return split(w[pl.ds(pl.multiple_of(i * n, n), n), :])

    mine, given = rows_of(ir, own_r), rows_of(ir ^ 1, own_r)
    tall = jnp.concatenate([mine[0], given[0], mine[1], given[1]], axis=0)
    start = (ir % 2) * cols
    tile = 512
    for j in range(cols // tile):
        high, low = split(z[tile * j : tile * (j + 1), :])
        both = mm(tall, high, NT)
        both = both[: 2 * own_r] + both[2 * own_r :] + mm(tall[: 2 * own_r], low, NT)
        there = pl.ds(pl.multiple_of(start + tile * j, tile), tile)
        projected_ref[:, there] = both[:own_r]
        given_ref[:, tile * j : tile * (j + 1)] = both[own_r:].astype(BF16)
    both = mm(jnp.concatenate(rows_of(ic, own_c), axis=0), s[...], NT)
    basis_ref[...] = both[:own_c] + both[own_c:]


def final_call(groups, done, early, y2, gram, z, places, quarter, depth, own_r, own_c):
    columns = gram.shape[0]
    parts = [a for group in groups for a in group]
    counts = [len(group) for group in groups]
    height = quarter * len(places)
    tall = sum(a.shape[0] for a in groups[0]) // (quarter + depth) * quarter
    cols = y2.shape[0]
    return pl.pallas_call(
        lambda *refs: final_kernel(places, depth, done, early, counts, *refs),
        out_shape=[
            jax.ShapeDtypeStruct((own_c, height), F32),
            jax.ShapeDtypeStruct((own_r, 2 * cols), F32),
            jax.ShapeDtypeStruct((own_r, cols), BF16),
        ],
        scratch_shapes=[
            pltpu.VMEM((columns, columns), F32),
            pltpu.VMEM((height, columns), BF16),
            pltpu.VMEM((cols, columns), F32),
            pltpu.VMEM((len(groups) - done, tall, y2.shape[1]), BF16),
        ],
        compiler_params=pltpu.CompilerParams(vmem_limit_bytes=40 * 2**20),
        name="factor_and_project",
    )(*parts, y2, gram, z)


def swap(a, axis, bits):
    return lax.ppermute(a, axis, [(i, i ^ bits) for i in range(lax.axis_size(axis))])


def local(row_features, col_features, test_block):
    cols = lax.axis_size("cols")
    rows = lax.axis_size("rows")
    chips_y, chips_z = cols // 2, rows // 2
    ir = lax.axis_index("rows")
    height, width = row_features.shape
    scale = 1.0 / math.sqrt(width)
    columns = test_block.shape[1]
    half = height // 2
    quarter = half // chips_y

    x_t, y_t = row_features.T, col_features.T
    depth = max(16, quarter * width // columns)
    x_own, s_own, *given = sketch_call(x_t, y_t, test_block, scale, quarter, depth)
    y2 = columns_call(y_t)
    there = []
    for bits, a in list(enumerate(given, 1))[::-1]:
        there.append(swap(a, "cols", bits))
    x_own, s_own = hold_call(x_own, s_own)
    piece = piece_call(x_own, [s_own] + there)

    along_z = {0: piece}
    for d in range(1, chips_z):
        along_z[d] = swap(piece, "rows", 2 * d)
    own = jnp.concatenate([along_z[d] for d in range(chips_z)], 0)
    near_x = swap(own, "rows", 1)
    near_y = [swap(own, "cols", 2 * d) for d in range(1, chips_y)]
    own_core = swap(own, "cols", 1)
    gram = gram_call([own, own_core], quarter, depth)
    z = product_call([own], y2, quarter, depth)
    z = product_call([own_core], y2, quarter, depth, z)
    cut = own.shape[0] // 2
    far = []
    for d in range(1, chips_y):
        low = swap(near_y[d - 1][:cut], "rows", 1)
        far.append([low, swap(near_x[cut:], "cols", 2 * d)])
    near = [near_x] + near_y
    near_core = [swap(a, "cols", 1) for a in near]
    gram = gram_call(near + near_core, quarter, depth, gram)
    z = product_call(near, y2, quarter, depth, z)
    singles = [own, own_core] + near + near_core
    done = 2 + len(near)
    early = len(singles)
    groups = [[a] for a in singles] + far + [[swap(a, "cols", 1) for a in pair] for pair in far]

    places = []
    with_y = len(near)
    for k, group in enumerate(
        (
            [0] + list(range(3, 2 + with_y)),
            [1] + list(range(3 + with_y, 2 + 2 * with_y)),
        )
    ):
        for d, n in enumerate(group):

            def place(k=k, d=d):
                c = lax.axis_index("cols")
                return ((c % 2) ^ k) * chips_y + ((c // 2) ^ d)

            places.append((place, n))
    basis_t, projected, given = final_call(
        groups, done, early, y2, gram, z, places, quarter, depth, columns // rows, columns // cols
    )
    there = swap(given, "rows", 1).astype(F32)
    projected = lax.dynamic_update_slice_in_dim(
        projected, there, (1 - ir % 2) * there.shape[1], 1
    )
    return (basis_t.T, projected)


def solution(mesh):
    in_specs = (P("rows", None), P("cols", None), P("cols", None))
    out_specs = (P("rows", "cols"), P("rows", "cols"))
    return jax.shard_map(local, mesh=mesh, in_specs=in_specs, out_specs=out_specs, check_vma=False)
```
